32 devices in a mesh: dp: 8 (over y, x, core), mem: 4 (over z).
Axes of the slice: x: 2, y: 2, z: 4, core: 2. Of those that a mesh axis runs over, the one named last changes fastest.
Arguments:
- target_in: bfloat16 [2, 32, 256, 1024], P(None, ('dp', 'mem')), may hold values from -45 to 45
- memory: bfloat16 [2, 32, 1024, 1024], P(None, 'dp', 'mem'), may hold values from -6 to 6
- target_len: int32 [2, 32], P(None, ('dp', 'mem')), may hold values from 64 to 256, as said below
- mem_len: int32 [2, 32], P(None, ('dp', 'mem')), may hold values from 512 to 1024, as said below
- cotangent: bfloat16 [2, 32, 256, 1024], P(None, ('dp', 'mem')), may hold values from -6 to 6
- gain_self: float32 [1024], replicated, may hold values from 0.5 to 1.5
- gain_cross: float32 [1024], replicated, may hold values from 0.5 to 1.5
- gain_ffn: float32 [1024], replicated, may hold values from 0.5 to 1.5
- rel_table: float32 [32, 16], replicated, may hold values from -4 to 4
- w_query: bfloat16 [1024, 1024], replicated, may hold values from -0.0234375 to 0.0234375
- w_key: bfloat16 [1024, 512], replicated, may hold values from -0.1875 to 0.1875
- w_value: bfloat16 [1024, 512], replicated, may hold values from -0.1875 to 0.1875
- w_out: bfloat16 [1024, 1024], replicated, may hold values from -1.5 to 1.5
- c_query: bfloat16 [1024, 1024], replicated, may hold values from -0.0234375 to 0.0234375
- c_key: bfloat16 [1024, 512], replicated, may hold values from -0.1875 to 0.1875
- c_value: bfloat16 [1024, 512], replicated, may hold values from -0.1875 to 0.1875
- c_out: bfloat16 [1024, 1024], replicated, may hold values from -3 to 3
- w_gate: bfloat16 [1024, 2816], replicated, may hold values from -0.1875 to 0.1875
- w_up: bfloat16 [1024, 2816], replicated, may hold values from -0.1875 to 0.1875
- w_down: bfloat16 [2816, 1024], replicated, may hold values from -0.109375 to 0.109375
Outputs:
- out: bfloat16 [2, 32, 256, 1024], P(None, ('dp', 'mem'))
- target_grad: bfloat16 [2, 32, 256, 1024], P(None, ('dp', 'mem'))
- memory_grad: bfloat16 [2, 32, 1024, 1024], P(None, 'dp', 'mem')
- grad_gain_self: float32 [1024], replicated
- grad_gain_cross: float32 [1024], replicated
- grad_gain_ffn: float32 [1024], replicated
- grad_rel_table: float32 [32, 16], replicated
- grad_w_query: float32 [1024, 1024], P(('dp', 'mem'))
- grad_w_key: float32 [1024, 512], P(('dp', 'mem'))
- grad_w_value: float32 [1024, 512], P(('dp', 'mem'))
- grad_w_out: float32 [1024, 1024], P(('dp', 'mem'))
- grad_c_query: float32 [1024, 1024], P(('dp', 'mem'))
- grad_c_key: float32 [1024, 512], P(('dp', 'mem'))
- grad_c_value: float32 [1024, 512], P(('dp', 'mem'))
- grad_c_out: float32 [1024, 1024], P(('dp', 'mem'))
- grad_w_gate: float32 [1024, 2816], P(('dp', 'mem'))
- grad_w_up: float32 [1024, 2816], P(('dp', 'mem'))
- grad_w_down: float32 [2816, 1024], P(('dp', 'mem'))
The draws below stay inside these ranges and needn't reach their ends.
Inputs may be any that keep to these rules, and one draw needn't show every extreme that they name: `target_len`: in every micro-batch one sequence has exactly 256 live target positions and another exactly a quarter of 256. `mem_len`: in every micro-batch one sequence has exactly 1024 live memory positions and another exactly half of 1024.
All inputs are finite; a program needn't handle non-finite values.
Results may differ from the reference program's by a relative error of at most 0.019.
Values may be sent and summed in bfloat16 or wider, within the bound.
No kernel may reach another device: no remote copies, remote signals or barrier semaphores. Data moves between devices by JAX's collectives and lax.ppermute only.
A program may use at most 384 MiB of HBM per device.

```python
import jax
import jax.numpy as jnp
import numpy as np
from jax import lax

D = 1024
QUERY_HEADS = 16
HEAD_SIZE = 64
KEY_VALUE_HEADS = 8
FF = 2816
NB = 32
MAXD = 128
TLEN = 256
MLEN = 1024
MB = 2
HQ = 1024
KV = 512
SEQS = 32


def ragged(key, lowest, highest):
    counts = jax.random.randint(key, (MB, SEQS), lowest, highest + 1)
    first = jax.random.randint(jax.random.fold_in(key, 3), (MB,), 0, SEQS)
    other = (first + 1 + jax.random.randint(jax.random.fold_in(key, 5), (MB,), 0, SEQS - 1)) % SEQS
    column = jnp.arange(SEQS)[None, :]
    counts = jnp.where(column == first[:, None], highest, counts)
    counts = jnp.where(column == other[:, None], lowest, counts)
    return counts.astype(jnp.int32)


def draw_target_len(key, part):
    return ragged(jax.random.fold_in(key, 11), TLEN // 4, TLEN)


def draw_mem_len(key, part):
    return ragged(jax.random.fold_in(key, 13), MLEN // 2, MLEN)


def draw_target_in(key, part):
    base_key, row_key, col_key = jax.random.split(jax.random.fold_in(key, 17), 3)
    shape = (MB, SEQS, TLEN, D)
    base = jnp.clip(jax.random.normal(base_key, shape, jnp.float32), -4.0, 4.0)
    row_scale = jnp.exp(jax.random.uniform(row_key, (MB, SEQS, TLEN, 1), jnp.float32, -1.2, 1.2))
    col_scale = jnp.exp(jax.random.uniform(col_key, (D,), jnp.float32, -1.2, 1.2))
    return (base * row_scale * col_scale).astype(jnp.bfloat16)


def levels(stream_key, dims, pieces, low, largest):
    level, own = 1.0, jax.random.fold_in(stream_key, 6)
    for dim, parts in pieces:
        draws = jnp.exp(jax.random.uniform(jax.random.fold_in(own, dim), (parts,), jnp.float32, low / len(pieces), largest / len(pieces)))
        level = level * jnp.repeat(draws, dims[dim] // parts).reshape([-1 if axis == dim else 1 for axis in range(len(dims))])
    return level


def noise(stream_key, shape, width, limit, cuts=(), kind=jnp.bfloat16):
    array = jax.random.normal(stream_key, shape, jnp.float32) * width
    if len(cuts) > 0:
        array = levels(stream_key, shape, cuts, -0.22, 0.18) * array
    return jnp.clip(array, min=-limit, max=limit).astype(kind)


def setup_inputs(seed: int = 0) -> dict:
    arg_keys = jax.random.split(jax.random.key(seed), 21)
    target_in = draw_target_in(jax.random.fold_in(arg_keys[20], 71), 0)
    memory = noise(arg_keys[1], (MB, SEQS, MLEN, D), 1.0, 6.0, ((1, 8), (2, 4)))
    target_len = draw_target_len(jax.random.fold_in(arg_keys[20], 71), 0)
    mem_len = draw_mem_len(jax.random.fold_in(arg_keys[20], 71), 0)
    cotangent = noise(arg_keys[4], (MB, SEQS, TLEN, D), 1.0, 6.0, ((1, 32),))
    gain_self = jnp.clip(1.0 + 0.1 * jax.random.normal(arg_keys[5], (D,), jnp.float32), 0.5, 1.5)
    gain_cross = jnp.clip(1.0 + 0.1 * jax.random.normal(arg_keys[6], (D,), jnp.float32), 0.5, 1.5)
    gain_ffn = jnp.clip(1.0 + 0.1 * jax.random.normal(arg_keys[7], (D,), jnp.float32), 0.5, 1.5)
    rel_table = noise(arg_keys[8], (NB, QUERY_HEADS), 1.0, 4.0, (), jnp.float32)
    w_query = noise(arg_keys[9], (D, HQ), (D * HEAD_SIZE) ** -0.5, 0.0234375)
    w_key = noise(arg_keys[10], (D, KV), D ** -0.5, 0.1875)
    w_value = noise(arg_keys[11], (D, KV), D ** -0.5, 0.1875)
    w_out = noise(arg_keys[12], (HQ, D), (max(1, HQ // 64)) ** -0.5, 1.5)
    c_query = noise(arg_keys[13], (D, HQ), (D * HEAD_SIZE) ** -0.5, 0.0234375)
    c_key = noise(arg_keys[14], (D, KV), D ** -0.5, 0.1875)
    c_value = noise(arg_keys[15], (D, KV), D ** -0.5, 0.1875)
    c_out = noise(arg_keys[16], (HQ, D), (max(1, HQ // 256)) ** -0.5, 3.0)
    w_gate = noise(arg_keys[17], (D, FF), D ** -0.5, 0.1875)
    w_up = noise(arg_keys[18], (D, FF), D ** -0.5, 0.1875)
    w_down = noise(arg_keys[19], (FF, D), FF ** -0.5, 0.109375)
    return dict(target_in=target_in, memory=memory, target_len=target_len, mem_len=mem_len, cotangent=cotangent, gain_self=gain_self, gain_cross=gain_cross, gain_ffn=gain_ffn, rel_table=rel_table, w_query=w_query, w_key=w_key, w_value=w_value, w_out=w_out, c_query=c_query, c_key=c_key, c_value=c_value, c_out=c_out, w_gate=w_gate, w_up=w_up, w_down=w_down)


EPSILON = 1e-06
MASKED = -1e+30
EXACT_PRECISION = lax.Precision.HIGHEST

@jax.custom_vjp
def low(v):
    return lax.optimization_barrier(v.astype(jnp.bfloat16)).astype(jnp.float32)

@jax.custom_vjp
def low_back(v):
    return v

def low_keep(v):
    return (low(v), None)

def low_pass(kept, grad):
    return (grad,)

def back_keep(v):
    return (v, None)

def back_low(kept, grad):
    return (low(grad),)
low.defvjp(low_keep, low_pass)
low_back.defvjp(back_keep, back_low)

def bucket_onehot(length):
    half = NB // 2
    distance = np.arange(length)
    spread = np.floor(np.log(np.maximum(distance, half) / half) / np.log(MAXD / half) * half)
    chosen = np.where(distance < half, distance, np.minimum(spread + half, NB - 1))
    return jnp.asarray(np.where(chosen[None, :] == np.arange(NB)[:, None], 1.0, 0.0), jnp.float32)

def offsets_of(length):
    return jnp.asarray(np.maximum(np.arange(length)[:, None] - np.arange(length)[None, :], 0), jnp.int32)

def normed(value_rows, gain):
    return value_rows * lax.rsqrt(lax.optimization_barrier(jnp.mean(value_rows * value_rows, axis=-1, keepdims=True)) + EPSILON) * gain

def rounded(value_rows):
    return low(low_back(value_rows))

def product(left, right):
    return jnp.dot(left, right, precision=EXACT_PRECISION)

def attend(query_rows, key_rows, value_rows, bias, keep):
    row_count, column_count = (query_rows.shape[0], key_rows.shape[0])
    shared_heads = QUERY_HEADS // KEY_VALUE_HEADS
    score_matrix = jnp.einsum('cpji,qpi->pjcq', query_rows.reshape(row_count, KEY_VALUE_HEADS, shared_heads, HEAD_SIZE), key_rows.reshape(column_count, KEY_VALUE_HEADS, HEAD_SIZE), precision=EXACT_PRECISION)
    score_matrix = low_back(score_matrix.reshape(QUERY_HEADS, row_count, column_count) + bias)
    probabilities = low(jax.nn.softmax(jnp.where(keep, score_matrix, MASKED), axis=-1))
    mixed_output = jnp.einsum('hwpy,yhi->phwi', probabilities.reshape(KEY_VALUE_HEADS, shared_heads, row_count, column_count), value_rows.reshape(column_count, KEY_VALUE_HEADS, HEAD_SIZE), precision=EXACT_PRECISION)
    return mixed_output.reshape(row_count, QUERY_HEADS * HEAD_SIZE)

def decoder_layer(params, inputs, encoded, target_count, memory_count):
    gain_self, gain_cross, gain_ffn, rel_table, w_query, w_key, w_value, w_out, c_query, c_key, c_value, c_out, w_gate, w_up, w_down = params
    position = jnp.arange(TLEN)
    bias = jnp.take(jnp.dot(rel_table.T, bucket_onehot(TLEN), precision=EXACT_PRECISION), offsets_of(TLEN), axis=1)
    self_keep = (position[None, :] <= position[:, None]) & (position[None, :] < target_count)
    cross_keep = (jnp.arange(MLEN) < memory_count)[None, :]
    normed_self = low(normed(inputs, gain_self))
    query_rows = rounded(product(normed_self, w_query))
    key_rows = rounded(product(normed_self, w_key))
    value_rows = rounded(product(normed_self, w_value))
    attended = rounded(attend(query_rows, key_rows, value_rows, bias, self_keep[None]))
    after_self = inputs + low_back(product(attended, w_out))
    normed_cross = low(normed(after_self, gain_cross))
    cross_queries = rounded(product(normed_cross, c_query))
    cross_keys = rounded(product(encoded, c_key))
    cross_values = rounded(product(encoded, c_value))
    cross_mixed = rounded(attend(cross_queries, cross_keys, cross_values, 0.0, cross_keep[None]))
    after_cross = after_self + low_back(product(cross_mixed, c_out))
    normed_ffn = low(normed(after_cross, gain_ffn))
    gate = low_back(product(normed_ffn, w_gate))
    upward = low_back(product(normed_ffn, w_up))
    hidden = low(jax.nn.gelu(gate, approximate=True) * upward)
    result = after_cross + low_back(product(hidden, w_down))
    return jnp.where((position < target_count)[:, None], result, 0.0)

def reference(target_in, memory, target_len, mem_len, cotangent, gain_self, gain_cross, gain_ffn, rel_table, w_query, w_key, w_value, w_out, c_query, c_key, c_value, c_out, w_gate, w_up, w_down):
    params = tuple((item.astype(jnp.float32) for item in (gain_self, gain_cross, gain_ffn, rel_table, w_query, w_key, w_value, w_out, c_query, c_key, c_value, c_out, w_gate, w_up, w_down)))
    count = MB * SEQS
    items = (target_in.reshape(count, TLEN, D), memory.reshape(count, MLEN, D), target_len.reshape(count), mem_len.reshape(count), cotangent.reshape(count, TLEN, D))

    def visit(totals, item):
        inputs, encoded, target_count, memory_count, grad_out = item

        def runner(weight_matrices, row_count, memory_rows):
            return decoder_layer(weight_matrices, row_count, memory_rows, target_count, memory_count)
        result, pull = jax.vjp(runner, params, inputs.astype(jnp.float32), encoded.astype(jnp.float32))
        grad_params, grad_inputs, grad_memory = pull(grad_out.astype(jnp.float32))
        totals = jax.tree.map(jnp.add, totals, grad_params)
        return (totals, (result.astype(jnp.bfloat16), grad_inputs.astype(jnp.bfloat16), grad_memory.astype(jnp.bfloat16)))
    zeros = jax.tree.map(jnp.zeros_like, params)
    totals, (results, input_grads, memory_grads) = lax.scan(visit, zeros, items)
    return (results.reshape(MB, SEQS, TLEN, D), input_grads.reshape(MB, SEQS, TLEN, D), memory_grads.reshape(MB, SEQS, MLEN, D), totals[0], totals[1], totals[2], totals[3], totals[4], totals[5], totals[6], totals[7], totals[8], totals[9], totals[10], totals[11], totals[12], totals[13], totals[14])
```

```python
import functools

import jax
import jax.numpy as jnp
import numpy as np
from jax import lax
from jax.experimental import pallas as pl
from jax.experimental.pallas import tpu as pltpu
from jax.sharding import PartitionSpec as P

QUERY_HEADS = 16
HEAD_SIZE = 64
KEY_VALUE_HEADS = 8
NB = 32
MAXD = 128
SHARED = QUERY_HEADS // KEY_VALUE_HEADS
PAIR = 2
PAIRS = KEY_VALUE_HEADS // PAIR
STEP_HEADS = PAIR * SHARED

EPSILON = 1e-06
MASKED = -1e30
EXACT_PRECISION = lax.Precision.HIGHEST


def bucket_index(length):
    half = NB // 2
    distance = np.arange(length)
    spread = np.floor(np.log(np.maximum(distance, half) / half) / np.log(MAXD / half) * half)
    return np.where(distance < half, distance, np.minimum(spread + half, NB - 1)).astype(np.int64)


def bucket_onehot(length):
    chosen = bucket_index(length)
    return np.where(chosen[None, :] == np.arange(NB)[:, None], 1.0, 0.0).astype(np.float32)


def inverse_rms(rows):
    return lax.rsqrt(jnp.mean(rows * rows, axis=-1, keepdims=True) + EPSILON)


def normed(rows, gain):
    return (rows * inverse_rms(rows) * gain).astype(jnp.bfloat16)


def norm_back(rows, gain, gradient):
    scale = inverse_rms(rows)
    scaled = gradient * gain
    shared = jnp.mean(scaled * rows, axis=-1, keepdims=True)
    part_rows = scale * scaled - rows * (scale * scale * scale * shared)
    return part_rows, jnp.sum(gradient * rows * scale, axis=0)


def dot32(left, right, dims):
    return lax.dot_general(left, right, (dims, ((), ())), preferred_element_type=jnp.float32)


def multiply(left, right):
    return dot32(left, right, ((1,), (0,)))


def outer_sum(left, right):
    return dot32(left, right, ((0,), (0,)))


def times_transposed(left, right):
    return dot32(left, right, ((1,), (1,)))


def head_rows(ref_rows, key_head):
    first = key_head * SHARED * HEAD_SIZE
    return jnp.concatenate(
        [ref_rows[:, first + i * HEAD_SIZE : first + (i + 1) * HEAD_SIZE] for i in range(SHARED)],
        axis=0,
    )


def head_columns(rows, length):
    return [rows[i * length : (i + 1) * length] for i in range(SHARED)]


def store_log_totals(lse_ref, columns):
    length = columns[0].shape[0]
    lane = lax.broadcasted_iota(jnp.int32, (length, 128), 1)
    packed = jnp.zeros((length, 128), jnp.float32)
    for index, column in enumerate(columns):
        packed = jnp.where(lane == index, column, packed)
    lse_ref[0, 0] = jnp.transpose(packed)[:8]


def self_forward_kernel(count_ref, q_ref, k_ref, v_ref, base_ref, out_ref, lse_ref):
    length = q_ref.shape[0]
    count = count_ref[pl.program_id(0)]
    row = lax.broadcasted_iota(jnp.int32, (length, length), 0)
    column = lax.broadcasted_iota(jnp.int32, (length, length), 1)
    keep = (column <= row) & (column < count)
    keep = jnp.concatenate([keep.astype(jnp.float32)] * SHARED, axis=0) > 0.5
    outs, totals = [], []
    for j in range(PAIR):
        queries = head_rows(q_ref, j)
        keys = k_ref[:, j * HEAD_SIZE : (j + 1) * HEAD_SIZE]
        values = v_ref[:, j * HEAD_SIZE : (j + 1) * HEAD_SIZE]
        bias = jnp.concatenate(
            [
                pltpu.roll(
                    jnp.broadcast_to(base_ref[0, j * SHARED + i : j * SHARED + i + 1, :], (length, length)),
                    0,
                    1,
                    stride=1,
                    stride_axis=0,
                )
                for i in range(SHARED)
            ],
            axis=0,
        )
        scores = jnp.where(keep, times_transposed(queries, keys) + bias, MASKED)
        highest = jnp.max(scores, axis=-1, keepdims=True)
        terms = jnp.exp(scores - highest)
        total = jnp.sum(terms, axis=-1, keepdims=True)
        mixed = multiply(terms.astype(jnp.bfloat16), values) / total
        outs += head_columns(mixed, length)
        totals += head_columns(highest + jnp.log(total), length)
    out_ref[...] = jnp.concatenate(outs, axis=1).astype(jnp.bfloat16)
    store_log_totals(lse_ref, totals)


def diagonal_sums(square):
    length = square.shape[0]
    group = 8
    total = square[:group]
    for first in range(group, length, group):
        total = total + pltpu.roll(square[first : first + group], length - first, 1)
    row = lax.broadcasted_iota(jnp.int32, (group, length), 0)
    sums = jnp.where(row == 0, total, 0.0)
    for r in range(1, group):
        sums = sums + jnp.where(row == r, pltpu.roll(total, length - r, 1), 0.0)
    return jnp.sum(sums, axis=0, keepdims=True)


def self_backward_kernel(
    count_ref, q_ref, k_ref, v_ref, g_ref, lse_ref, base_ref, dq_ref, dk_ref, dv_ref, diag_ref
):
    length = q_ref.shape[0]
    count = count_ref[pl.program_id(0)]
    row = lax.broadcasted_iota(jnp.int32, (length, length), 0)
    column = lax.broadcasted_iota(jnp.int32, (length, length), 1)
    keep = (row <= column) & (row < count)
    dqs, dks, dvs, diagonals = [], [], [], []
    for j in range(PAIR):
        queries = head_rows(q_ref, j)
        gradient = head_rows(g_ref, j)
        keys = k_ref[:, j * HEAD_SIZE : (j + 1) * HEAD_SIZE]
        values = v_ref[:, j * HEAD_SIZE : (j + 1) * HEAD_SIZE]
        scores_all = times_transposed(keys, queries)
        grad_all = times_transposed(values, gradient)
        weights, score_grads = [], []
        for i in range(SHARED):
            h = j * SHARED + i
            bias = pltpu.roll(
                jnp.broadcast_to(base_ref[0, h : h + 1, :], (length, length)),
                0,
                1,
                stride=1,
                stride_axis=0,
            )
            scores = scores_all[:, i * length : (i + 1) * length] + bias
            scores = jnp.where(keep, scores, MASKED)
            probs = jnp.exp(scores - lse_ref[0, 0, h : h + 1, :])
            weights.append(probs.astype(jnp.bfloat16))
            product = probs * grad_all[:, i * length : (i + 1) * length]
            centre = jnp.sum(product, axis=0, keepdims=True)
            score_grad = (product - probs * centre).astype(jnp.bfloat16)
            score_grads.append(score_grad)
            diagonals.append(diagonal_sums(score_grad.astype(jnp.float32)))
        weights = jnp.concatenate(weights, axis=1)
        score_grads = jnp.concatenate(score_grads, axis=1)
        dvs.append(multiply(weights, gradient))
        dks.append(multiply(score_grads, queries))
        dq = jnp.transpose(outer_sum(keys, score_grads))
        dqs += head_columns(dq, length)
    dq_ref[...] = jnp.concatenate(dqs, axis=1).astype(jnp.bfloat16)
    dk_ref[...] = jnp.concatenate(dks, axis=1).astype(jnp.bfloat16)
    dv_ref[...] = jnp.concatenate(dvs, axis=1).astype(jnp.bfloat16)
    diag_ref[0, 0] = jnp.concatenate(diagonals, axis=0)


def cross_forward_kernel(chunks, count_ref, base_ref, q_ref, *refs):
    k_refs, v_refs = refs[:chunks], refs[chunks : 2 * chunks]
    out_ref, lse_ref, score_ref = refs[2 * chunks :]
    length, rows = q_ref.shape[0], k_refs[0].shape[1]
    count = count_ref[pl.program_id(0)]
    column = lax.broadcasted_iota(jnp.int32, (1, rows), 1)
    outs, totals = [], []
    for j in range(PAIR):
        queries = head_rows(q_ref, j)
        highest = None
        for c in range(chunks):
            keys = k_refs[c][0, :, j * HEAD_SIZE : (j + 1) * HEAD_SIZE]
            scores = jnp.where(
                column + base_ref[c] < count, times_transposed(queries, keys), MASKED
            )
            score_ref[c] = scores
            top = jnp.max(scores, axis=-1, keepdims=True)
            highest = top if highest is None else jnp.maximum(highest, top)
        total, mixed = 0.0, 0.0
        for c in range(chunks):
            values = v_refs[c][0, :, j * HEAD_SIZE : (j + 1) * HEAD_SIZE]
            terms = jnp.exp(score_ref[c] - highest)
            total = total + jnp.sum(terms, axis=-1, keepdims=True)
            mixed = mixed + multiply(terms.astype(jnp.bfloat16), values)
        outs += head_columns(mixed / total, length)
        totals += head_columns(highest + jnp.log(total), length)
    out_ref[...] = jnp.concatenate(outs, axis=1).astype(jnp.bfloat16)
    store_log_totals(lse_ref, totals)


def cross_backward_kernel(chunks, count_ref, base_ref, q_ref, g_ref, lse_ref, *refs):
    k_refs, v_refs = refs[:chunks], refs[chunks : 2 * chunks]
    dq_ref = refs[2 * chunks]
    d_refs = refs[2 * chunks + 1 : 3 * chunks + 1]
    probs_ref, product_ref = refs[3 * chunks + 1 :]
    length, rows = q_ref.shape[0], k_refs[0].shape[1]
    half = d_refs[0].shape[2] // 2
    count = count_ref[pl.program_id(0)]
    first = pl.program_id(1) * (PAIR * HEAD_SIZE)
    position = lax.broadcasted_iota(jnp.int32, (rows, 1), 0)
    dqs = []
    dks, dvs = [[] for _ in range(chunks)], [[] for _ in range(chunks)]
    for j in range(PAIR):
        queries = head_rows(q_ref, j)
        gradient = head_rows(g_ref, j)
        log_total = jnp.concatenate(
            [lse_ref[0, 0, j * SHARED + i : j * SHARED + i + 1, :] for i in range(SHARED)], axis=1
        )
        centre = 0.0
        for c in range(chunks):
            keys = k_refs[c][0, :, j * HEAD_SIZE : (j + 1) * HEAD_SIZE]
            values = v_refs[c][0, :, j * HEAD_SIZE : (j + 1) * HEAD_SIZE]
            scores = jnp.where(
                position + base_ref[c] < count, times_transposed(keys, queries), MASKED
            )
            probs = jnp.exp(scores - log_total)
            product = probs * times_transposed(values, gradient)
            centre = centre + jnp.sum(product, axis=0, keepdims=True)
            dvs[c].append(multiply(probs.astype(jnp.bfloat16), gradient))
            probs_ref[c] = probs
            product_ref[c] = product
        dq = 0.0
        for c in range(chunks):
            keys = k_refs[c][0, :, j * HEAD_SIZE : (j + 1) * HEAD_SIZE]
            score_grad = (product_ref[c] - probs_ref[c] * centre).astype(jnp.bfloat16)
            dks[c].append(multiply(score_grad, queries))
            dq = dq + outer_sum(keys, score_grad)
        dqs += head_columns(jnp.transpose(dq), length)
    dq_ref[...] = jnp.concatenate(dqs, axis=1).astype(jnp.bfloat16)
    for c in range(chunks):
        d_refs[c][0, :, pl.ds(pl.multiple_of(first, 128), 128)] = jnp.concatenate(
            dks[c], axis=1
        ).astype(jnp.bfloat16)
        d_refs[c][0, :, pl.ds(pl.multiple_of(half + first, 128), 128)] = jnp.concatenate(
            dvs[c], axis=1
        ).astype(jnp.bfloat16)


def feed_forward_kernel(
    n_ref, b_ref, wg_ref, wu_ref, wd_ref, hid_ref, gg_ref, gu_ref, y_ref, gn_ref
):
    root = float(np.sqrt(2.0 / np.pi))

    @pl.when(pl.program_id(0) == 0)
    def _():
        y_ref[...] = jnp.zeros_like(y_ref)
        gn_ref[...] = jnp.zeros_like(gn_ref)

    gate = multiply(n_ref[...], wg_ref[...])
    upward = multiply(n_ref[...], wu_ref[...])
    back = times_transposed(b_ref[...], wd_ref[...])
    square = gate * gate
    bend = jnp.tanh(root * gate * (1.0 + 0.044715 * square))
    half_sum = 0.5 * (1.0 + bend)
    activated = gate * half_sum
    slope = half_sum + 0.5 * gate * (1.0 - bend * bend) * (root * (1.0 + 3 * 0.044715 * square))
    hidden = (activated * upward).astype(jnp.bfloat16)
    grad_gate = (back * upward * slope).astype(jnp.bfloat16)
    grad_upward = (back * activated).astype(jnp.bfloat16)
    hid_ref[...] = hidden
    gg_ref[...] = grad_gate
    gu_ref[...] = grad_upward
    y_ref[...] += multiply(hidden, wd_ref[...])
    gn_ref[...] += times_transposed(grad_gate, wg_ref[...]) + times_transposed(
        grad_upward, wu_ref[...]
    )


def shape(dims, dtype):
    return jax.ShapeDtypeStruct(tuple(dims), dtype)


def self_attention(q, k, v, counts, base):
    seqs, length = counts.shape[0], q.shape[0] // counts.shape[0]
    wide, narrow = STEP_HEADS * HEAD_SIZE, PAIR * HEAD_SIZE
    return pl.pallas_call(
        self_forward_kernel,
        out_shape=(shape(q.shape, jnp.bfloat16), shape((seqs, PAIRS, 8, length), jnp.float32)),
        grid_spec=pltpu.PrefetchScalarGridSpec(
            num_scalar_prefetch=1,
            grid=(seqs, PAIRS),
            in_specs=[
                pl.BlockSpec((length, wide), lambda s, p, _: (s, p)),
                pl.BlockSpec((length, narrow), lambda s, p, _: (s, p)),
                pl.BlockSpec((length, narrow), lambda s, p, _: (s, p)),
                pl.BlockSpec((1, STEP_HEADS, length), lambda s, p, _: (p, 0, 0)),
            ],
            out_specs=(
                pl.BlockSpec((length, wide), lambda s, p, _: (s, p)),
                pl.BlockSpec((1, 1, 8, length), lambda s, p, _: (s, p, 0, 0)),
            ),
        ),
        name="self_forward",
    )(counts, q, k, v, base)


def self_attention_back(q, k, v, counts, base, lse, gradient):
    seqs, length = counts.shape[0], q.shape[0] // counts.shape[0]
    wide, narrow = STEP_HEADS * HEAD_SIZE, PAIR * HEAD_SIZE
    return pl.pallas_call(
        self_backward_kernel,
        out_shape=(
            shape(q.shape, jnp.bfloat16),
            shape(k.shape, jnp.bfloat16),
            shape(v.shape, jnp.bfloat16),
            shape((seqs, PAIRS, STEP_HEADS, length), jnp.float32),
        ),
        grid_spec=pltpu.PrefetchScalarGridSpec(
            num_scalar_prefetch=1,
            grid=(seqs, PAIRS),
            in_specs=[
                pl.BlockSpec((length, wide), lambda s, p, _: (s, p)),
                pl.BlockSpec((length, narrow), lambda s, p, _: (s, p)),
                pl.BlockSpec((length, narrow), lambda s, p, _: (s, p)),
                pl.BlockSpec((length, wide), lambda s, p, _: (s, p)),
                pl.BlockSpec((1, 1, 8, length), lambda s, p, _: (s, p, 0, 0)),
                pl.BlockSpec((1, STEP_HEADS, length), lambda s, p, _: (p, 0, 0)),
            ],
            out_specs=(
                pl.BlockSpec((length, wide), lambda s, p, _: (s, p)),
                pl.BlockSpec((length, narrow), lambda s, p, _: (s, p)),
                pl.BlockSpec((length, narrow), lambda s, p, _: (s, p)),
                pl.BlockSpec((1, 1, STEP_HEADS, length), lambda s, p, _: (s, p, 0, 0)),
            ),
        ),
        name="self_backward",
    )(counts, q, k, v, gradient, lse, base)


def chunk_specs(pieces):
    rows, narrow = pieces[0].shape[1], PAIR * HEAD_SIZE
    keys = [pl.BlockSpec((1, rows, narrow), lambda s, p, *_: (s, 0, p)) for _ in pieces]
    values = [pl.BlockSpec((1, rows, narrow), lambda s, p, *_: (s, 0, PAIRS + p)) for _ in pieces]
    return keys + values


def cross_attention(q, pieces, counts, bases):
    seqs, length, rows = counts.shape[0], q.shape[0] // counts.shape[0], pieces[0].shape[1]
    wide = STEP_HEADS * HEAD_SIZE
    return pl.pallas_call(
        functools.partial(cross_forward_kernel, len(pieces)),
        out_shape=(shape(q.shape, jnp.bfloat16), shape((seqs, PAIRS, 8, length), jnp.float32)),
        grid_spec=pltpu.PrefetchScalarGridSpec(
            num_scalar_prefetch=2,
            grid=(seqs, PAIRS),
            in_specs=[pl.BlockSpec((length, wide), lambda s, p, *_: (s, p))] + chunk_specs(pieces),
            out_specs=(
                pl.BlockSpec((length, wide), lambda s, p, *_: (s, p)),
                pl.BlockSpec((1, 1, 8, length), lambda s, p, *_: (s, p, 0, 0)),
            ),
            scratch_shapes=[pltpu.VMEM((len(pieces), SHARED * length, rows), jnp.float32)],
        ),
        name="cross_forward",
    )(counts, bases, q, *pieces, *pieces)


def cross_attention_back(q, pieces, counts, bases, lse, gradient):
    seqs, length, rows = counts.shape[0], q.shape[0] // counts.shape[0], pieces[0].shape[1]
    wide, chunks = STEP_HEADS * HEAD_SIZE, len(pieces)
    return pl.pallas_call(
        functools.partial(cross_backward_kernel, chunks),
        out_shape=(shape(q.shape, jnp.bfloat16),)
        + tuple(shape(piece.shape, jnp.bfloat16) for piece in pieces),
        grid_spec=pltpu.PrefetchScalarGridSpec(
            num_scalar_prefetch=2,
            grid=(seqs, PAIRS),
            in_specs=[
                pl.BlockSpec((length, wide), lambda s, p, *_: (s, p)),
                pl.BlockSpec((length, wide), lambda s, p, *_: (s, p)),
                pl.BlockSpec((1, 1, 8, length), lambda s, p, *_: (s, p, 0, 0)),
            ]
            + chunk_specs(pieces),
            out_specs=(pl.BlockSpec((length, wide), lambda s, p, *_: (s, p)),)
            + tuple(
                pl.BlockSpec((1,) + piece.shape[1:], lambda s, p, *_: (s, 0, 0)) for piece in pieces
            ),
            scratch_shapes=[pltpu.VMEM((chunks, rows, SHARED * length), jnp.float32)] * 2,
        ),
        name="cross_backward",
    )(counts, bases, q, gradient, lse, *pieces, *pieces)


def feed_forward(rows_normed, branch, w_gate, w_up, w_down):
    rows, width = rows_normed.shape
    hidden = w_gate.shape[1]
    tile = 256
    return pl.pallas_call(
        feed_forward_kernel,
        out_shape=(shape((rows, hidden), jnp.bfloat16),) * 3
        + (shape((rows, width), jnp.float32),) * 2,
        grid=(hidden // tile,),
        in_specs=[
            pl.BlockSpec((rows, width), lambda f: (0, 0)),
            pl.BlockSpec((rows, width), lambda f: (0, 0)),
            pl.BlockSpec((width, tile), lambda f: (0, f)),
            pl.BlockSpec((width, tile), lambda f: (0, f)),
            pl.BlockSpec((tile, width), lambda f: (f, 0)),
        ],
        out_specs=(pl.BlockSpec((rows, tile), lambda f: (0, f)),) * 3
        + (pl.BlockSpec((rows, width), lambda f: (0, 0)),) * 2,
        name="feed_forward",
    )(rows_normed, branch, w_gate, w_up, w_down)


def bit_count(size):
    return size.bit_length() - 1


def reduce_rows(term, order):
    devices, members = lax.axis_size("dp"), lax.axis_size("mem")
    me, member = lax.axis_index("dp"), lax.axis_index("mem")
    bits = bit_count(devices)
    rows, columns = term.shape
    share = rows // (devices * members)
    current = term.reshape((2,) * bits + (members, share, columns))
    left = list(range(bits - 1, -1, -1))
    for bit in order:
        axis = left.index(bit)
        left.remove(bit)
        mine = (me >> bit) & 1
        sent = lax.dynamic_index_in_dim(current, 1 - mine, axis, keepdims=False)
        got = lax.ppermute(sent, "dp", [(i, i ^ (1 << bit)) for i in range(devices)])
        kept = lax.dynamic_index_in_dim(current, mine, axis, keepdims=False)
        current = (kept.astype(jnp.float32) + got.astype(jnp.float32)).astype(jnp.bfloat16)
    total = lax.dynamic_index_in_dim(current, member, 0, keepdims=False).astype(jnp.float32)
    for sign in (1, -1):
        got = None
        for step in range(members - 1):
            place = member if sign == 1 else members - 1 - member
            block = jnp.clip(members - 1 - step + place, 0, members - 1)
            block = block if sign == 1 else members - 1 - block
            sent = lax.dynamic_index_in_dim(current, block, 0, keepdims=False)
            if got is not None:
                sent = (sent.astype(jnp.float32) + got.astype(jnp.float32)).astype(jnp.bfloat16)
            pairs = [(i, i + 1) for i in range(step + 1)]
            if sign == -1:
                pairs = [(members - 1 - a, members - 1 - b) for a, b in pairs]
            got = lax.ppermute(sent, "mem", pairs)
        total = total + got.astype(jnp.float32)
    return total


def sum_everywhere(value):
    for axis in ("mem", "dp"):
        size = lax.axis_size(axis)
        for bit in range(bit_count(size)):
            value = value + lax.ppermute(value, axis, [(i, i ^ (1 << bit)) for i in range(size)])
    return value


def per_device(
    target_in,
    memory,
    target_len,
    mem_len,
    cotangent,
    gain_self,
    gain_cross,
    gain_ffn,
    rel_table,
    w_query,
    w_key,
    w_value,
    w_out,
    c_query,
    c_key,
    c_value,
    c_out,
    w_gate,
    w_up,
    w_down,
):
    micro, seqs, length, width = target_in.shape
    mem_rows = memory.shape[2]
    members, member = lax.axis_size("mem"), lax.axis_index("mem")
    devices = lax.axis_size("dp")
    bits = bit_count(devices)
    order_a = list(range(bits))
    order_b = [0] + order_a[:0:-1]
    count = micro * seqs
    key_width = c_key.shape[1]

    c_both = jnp.concatenate([c_key, c_value], axis=1)

    def block_of(array, shift):
        return lax.dynamic_slice_in_dim(array, lax.rem(member + shift, members) * seqs, seqs, 1)

    def shifted(array, shift):
        return lax.ppermute(
            array, "mem", [(i, (i + shift) % members) for i in range(members)]
        )

    pieces = []
    for shift in list(range(1, members)) + [0]:
        rows = block_of(memory, shift).reshape(count * mem_rows, width)
        both = multiply(rows, c_both).astype(jnp.bfloat16).reshape(count, mem_rows, -1)
        pieces.append(shifted(both, shift) if shift else both)
    pieces = [pieces[-1]] + pieces[:-1]
    bases = jnp.stack(
        [lax.rem(member + members - shift, members) * mem_rows for shift in range(members)]
    ).astype(jnp.int32)

    target_counts = target_len.reshape(count)
    memory_counts = mem_len.reshape(count)
    onehot = bucket_onehot(length)
    backwards = onehot[:, (-np.arange(length)) % length]
    base = jnp.dot(rel_table.T, jnp.asarray(onehot), precision=EXACT_PRECISION)
    base = base.reshape(PAIRS, STEP_HEADS, length)
    base_back = jnp.dot(rel_table.T, jnp.asarray(backwards), precision=EXACT_PRECISION)
    base_back = base_back.reshape(PAIRS, STEP_HEADS, length)

    inputs = target_in.reshape(count * length, width).astype(jnp.float32)
    normed_self = normed(inputs, gain_self)
    queries = multiply(normed_self, w_query).astype(jnp.bfloat16)
    keys = multiply(normed_self, w_key).astype(jnp.bfloat16)
    values = multiply(normed_self, w_value).astype(jnp.bfloat16)
    attended, self_lse = self_attention(queries, keys, values, target_counts, base_back)
    after_self = inputs + multiply(attended, w_out)
    normed_cross = normed(after_self, gain_cross)
    cross_queries = multiply(normed_cross, c_query).astype(jnp.bfloat16)
    cross_mixed, cross_lse = cross_attention(cross_queries, pieces, memory_counts, bases)
    after_cross = after_self + multiply(cross_mixed, c_out)
    normed_ffn = normed(after_cross, gain_ffn)

    position = jnp.arange(length)
    valid = (position[None, :] < target_counts[:, None]).reshape(count * length, 1)
    branch_ffn = jnp.where(valid, cotangent.reshape(count * length, width), 0)
    grad_result = branch_ffn.astype(jnp.float32)
    hidden, grad_gate, grad_upward, ffn_out, grad_normed = feed_forward(
        normed_ffn, branch_ffn, w_gate, w_up, w_down
    )
    out = jnp.where(valid, after_cross + ffn_out, 0.0).astype(jnp.bfloat16)

    def reduced(left, right, order):
        return reduce_rows(outer_sum(left, right).astype(jnp.bfloat16), order)

    half = width // 2
    g_gate = reduced(normed_ffn, grad_gate, order_a)
    g_up = reduced(normed_ffn, grad_upward, order_b)
    g_down_a = reduced(hidden, branch_ffn[:, :half], order_a)
    g_down_b = reduced(hidden, branch_ffn[:, half:], order_b)

    part, sum_gain_ffn = norm_back(after_cross, gain_ffn, grad_normed)
    grad_after_cross = grad_result + part
    branch_cross = grad_after_cross.astype(jnp.bfloat16)
    grad_cross_mixed = times_transposed(branch_cross, c_out).astype(jnp.bfloat16)
    found = cross_attention_back(
        cross_queries, pieces, memory_counts, bases, cross_lse, grad_cross_mixed
    )
    grad_cross_queries = found[0]
    grad_both = jnp.zeros((micro, memory.shape[1], mem_rows, 2 * key_width), jnp.bfloat16)
    for shift in range(members):
        piece = found[1 + shift]
        piece = shifted(piece, members - shift) if shift else piece
        grad_both = lax.dynamic_update_slice_in_dim(
            grad_both,
            piece.reshape(micro, seqs, mem_rows, -1),
            lax.rem(member + shift, members) * seqs,
            1,
        )
    grad_both = grad_both.reshape(-1, 2 * key_width)

    part, sum_gain_cross = norm_back(
        after_self, gain_cross, times_transposed(grad_cross_queries, c_query)
    )
    grad_after_self = grad_after_cross + part
    branch_self = grad_after_self.astype(jnp.bfloat16)
    grad_attended = times_transposed(branch_self, w_out).astype(jnp.bfloat16)

    g_c_out = reduced(cross_mixed, branch_cross, order_a)
    g_c_query = reduced(normed_cross, grad_cross_queries, order_b)

    grad_queries, grad_keys, grad_values, diagonals = self_attention_back(
        queries, keys, values, target_counts, base, self_lse, grad_attended
    )
    grad_normed = (
        times_transposed(grad_queries, w_query)
        + times_transposed(grad_keys, w_key)
        + times_transposed(grad_values, w_value)
    )
    part, sum_gain_self = norm_back(inputs, gain_self, grad_normed)
    target_grad = (grad_after_self + part).astype(jnp.bfloat16)
    distances = jnp.sum(diagonals, axis=0).reshape(QUERY_HEADS, length)
    table = jnp.dot(distances, jnp.asarray(onehot.T), precision=EXACT_PRECISION).T

    g_w_out = reduced(attended, branch_self, order_b)
    g_w_query = reduced(normed_self, grad_queries, order_a)
    g_w_key = reduced(normed_self, grad_keys, order_b)
    g_w_value = reduced(normed_self, grad_values, order_a)

    memory_grad = times_transposed(grad_both, c_both).astype(jnp.bfloat16).reshape(memory.shape)
    encoded = memory.reshape(-1, width)
    g_c_key = reduced(encoded, grad_both[:, :key_width], order_a)
    g_c_value = reduced(encoded, grad_both[:, key_width:], order_b)

    small = sum_everywhere(
        jnp.concatenate([sum_gain_self, sum_gain_cross, sum_gain_ffn, table.reshape(-1)])
    )
    return (
        out.reshape(micro, seqs, length, width),
        target_grad.reshape(micro, seqs, length, width),
        memory_grad,
        small[:width],
        small[width : 2 * width],
        small[2 * width : 3 * width],
        small[3 * width :].reshape(NB, QUERY_HEADS),
        g_w_query,
        g_w_key,
        g_w_value,
        g_w_out,
        g_c_query,
        g_c_key,
        g_c_value,
        g_c_out,
        g_gate,
        g_up,
        jnp.concatenate([g_down_a, g_down_b], axis=1),
    )


def solution(mesh):
    rows = P(None, ("dp", "mem"), None, None)
    lengths = P(None, ("dp", "mem"))
    encoded = P(None, "dp", "mem", None)
    return jax.shard_map(
        per_device,
        mesh=mesh,
        in_specs=(rows, encoded, lengths, lengths, rows) + (P(),) * 15,
        out_specs=(rows, rows, encoded) + (P(),) * 4 + (P(("dp", "mem"), None),) * 11,
        check_vma=False,
    )
```

```python
import functools

import jax
import jax.numpy as jnp
import numpy as np
from jax import lax
from jax.experimental import pallas as pl
from jax.experimental.pallas import tpu as pltpu
from jax.sharding import PartitionSpec as P


QUERY_HEADS = 16
HEAD_SIZE = 64
KEY_VALUE_HEADS = 8
NB = 32
MAXD = 128
SHARED = QUERY_HEADS // KEY_VALUE_HEADS
PAIR = 2
PAIRS = KEY_VALUE_HEADS // PAIR
STEP_HEADS = PAIR * SHARED

EPSILON = 1e-06
MASKED = -1e30
EXACT_PRECISION = lax.Precision.HIGHEST


def bucket_index(length):
    half = NB // 2
    distance = np.arange(length)
    spread = np.floor(np.log(np.maximum(distance, half) / half) / np.log(MAXD / half) * half)
    return np.where(distance < half, distance, np.minimum(spread + half, NB - 1)).astype(np.int64)


def bucket_onehot(length):
    chosen = bucket_index(length)
    return np.where(chosen[None, :] == np.arange(NB)[:, None], 1.0, 0.0).astype(np.float32)


def inverse_rms(rows):
    return lax.rsqrt(jnp.mean(rows * rows, axis=-1, keepdims=True) + EPSILON)


def normed(rows, gain):
    return (rows * inverse_rms(rows) * gain).astype(jnp.bfloat16)


def norm_back(rows, gain, gradient):
    scale = inverse_rms(rows)
    scaled = gradient * gain
    shared = jnp.mean(scaled * rows, axis=-1, keepdims=True)
    part_rows = scale * scaled - rows * (scale * scale * scale * shared)
    return part_rows, jnp.sum(gradient * rows * scale, axis=0)


def dot32(left, right, dims):
    return lax.dot_general(left, right, (dims, ((), ())), preferred_element_type=jnp.float32)


def multiply(left, right):
    return dot32(left, right, ((1,), (0,)))


def outer_sum(left, right):
    return dot32(left, right, ((0,), (0,)))


def times_transposed(left, right):
    return dot32(left, right, ((1,), (1,)))


def head_rows(ref_rows, key_head):
    first = key_head * SHARED * HEAD_SIZE
    return jnp.concatenate(
        [ref_rows[:, first + i * HEAD_SIZE : first + (i + 1) * HEAD_SIZE] for i in range(SHARED)],
        axis=0,
    )


def head_columns(rows, length):
    return [rows[i * length : (i + 1) * length] for i in range(SHARED)]


def store_log_totals(lse_ref, columns):
    length = columns[0].shape[0]
    lane = lax.broadcasted_iota(jnp.int32, (length, 128), 1)
    packed = jnp.zeros((length, 128), jnp.float32)
    for index, column in enumerate(columns):
        packed = jnp.where(lane == index, column, packed)
    lse_ref[0, 0] = jnp.transpose(packed)[:8]


def self_forward_kernel(count_ref, q_ref, k_ref, v_ref, base_ref, out_ref, lse_ref):
    length = q_ref.shape[0]
    count = count_ref[pl.program_id(0)]
    row = lax.broadcasted_iota(jnp.int32, (length, length), 0)
    column = lax.broadcasted_iota(jnp.int32, (length, length), 1)
    keep = (column <= row) & (column < count)
    keep = jnp.concatenate([keep.astype(jnp.float32)] * SHARED, axis=0) > 0.5
    outs, totals = [], []
    for j in range(PAIR):
        queries = head_rows(q_ref, j)
        keys = k_ref[:, j * HEAD_SIZE : (j + 1) * HEAD_SIZE]
        values = v_ref[:, j * HEAD_SIZE : (j + 1) * HEAD_SIZE]
        bias = jnp.concatenate(
            [
                pltpu.roll(
                    jnp.broadcast_to(base_ref[0, j * SHARED + i : j * SHARED + i + 1, :], (length, length)),
                    0,
                    1,
                    stride=1,
                    stride_axis=0,
                )
                for i in range(SHARED)
            ],
            axis=0,
        )
        scores = jnp.where(keep, times_transposed(queries, keys) + bias, MASKED)
        highest = jnp.max(scores, axis=-1, keepdims=True)
        terms = jnp.exp(scores - highest)
        total = jnp.sum(terms, axis=-1, keepdims=True)
        mixed = multiply(terms.astype(jnp.bfloat16), values) / total
        outs += head_columns(mixed, length)
        totals += head_columns(highest + jnp.log(total), length)
    out_ref[...] = jnp.concatenate(outs, axis=1).astype(jnp.bfloat16)
    store_log_totals(lse_ref, totals)


def diagonal_sums(square):
    length = square.shape[0]
    group = 8
    total = square[:group]
    for first in range(group, length, group):
        total = total + pltpu.roll(square[first : first + group], length - first, 1)
    row = lax.broadcasted_iota(jnp.int32, (group, length), 0)
    sums = jnp.where(row == 0, total, 0.0)
    for r in range(1, group):
        sums = sums + jnp.where(row == r, pltpu.roll(total, length - r, 1), 0.0)
    return jnp.sum(sums, axis=0, keepdims=True)


def self_backward_kernel(
    count_ref, q_ref, k_ref, v_ref, g_ref, lse_ref, base_ref, dq_ref, dk_ref, dv_ref, diag_ref
):
    length = q_ref.shape[0]
    count = count_ref[pl.program_id(0)]
    row = lax.broadcasted_iota(jnp.int32, (length, length), 0)
    column = lax.broadcasted_iota(jnp.int32, (length, length), 1)
    keep = (row <= column) & (row < count)
    dqs, dks, dvs, diagonals = [], [], [], []
    for j in range(PAIR):
        queries = head_rows(q_ref, j)
        gradient = head_rows(g_ref, j)
        keys = k_ref[:, j * HEAD_SIZE : (j + 1) * HEAD_SIZE]
        values = v_ref[:, j * HEAD_SIZE : (j + 1) * HEAD_SIZE]
        scores_all = times_transposed(keys, queries)
        grad_all = times_transposed(values, gradient)
        weights, score_grads = [], []
        for i in range(SHARED):
            h = j * SHARED + i
            bias = pltpu.roll(
                jnp.broadcast_to(base_ref[0, h : h + 1, :], (length, length)),
                0,
                1,
                stride=1,
                stride_axis=0,
            )
            scores = scores_all[:, i * length : (i + 1) * length] + bias
            scores = jnp.where(keep, scores, MASKED)
            probs = jnp.exp(scores - lse_ref[0, 0, h : h + 1, :])
            weights.append(probs.astype(jnp.bfloat16))
            product = probs * grad_all[:, i * length : (i + 1) * length]
            centre = jnp.sum(product, axis=0, keepdims=True)
            score_grad = (product - probs * centre).astype(jnp.bfloat16)
            score_grads.append(score_grad)
            diagonals.append(diagonal_sums(score_grad.astype(jnp.float32)))
        weights = jnp.concatenate(weights, axis=1)
        score_grads = jnp.concatenate(score_grads, axis=1)
        dvs.append(multiply(weights, gradient))
        dks.append(multiply(score_grads, queries))
        dq = jnp.transpose(outer_sum(keys, score_grads))
        dqs += head_columns(dq, length)
    dq_ref[...] = jnp.concatenate(dqs, axis=1).astype(jnp.bfloat16)
    dk_ref[...] = jnp.concatenate(dks, axis=1).astype(jnp.bfloat16)
    dv_ref[...] = jnp.concatenate(dvs, axis=1).astype(jnp.bfloat16)
    diag_ref[0, 0] = jnp.concatenate(diagonals, axis=0)


def cross_forward_kernel(chunks, count_ref, base_ref, q_ref, *refs):
    k_refs, v_refs = refs[:chunks], refs[chunks : 2 * chunks]
    out_ref, lse_ref, score_ref = refs[2 * chunks :]
    length, rows = q_ref.shape[0], k_refs[0].shape[1]
    count = count_ref[pl.program_id(0)]
    column = lax.broadcasted_iota(jnp.int32, (1, rows), 1)
    outs, totals = [], []
    for j in range(PAIR):
        queries = head_rows(q_ref, j)
        highest = None
        for c in range(chunks):
            keys = k_refs[c][0, :, j * HEAD_SIZE : (j + 1) * HEAD_SIZE]
            scores = jnp.where(
                column + base_ref[c] < count, times_transposed(queries, keys), MASKED
            )
            score_ref[c] = scores
            top = jnp.max(scores, axis=-1, keepdims=True)
            highest = top if highest is None else jnp.maximum(highest, top)
        total, mixed = 0.0, 0.0
        for c in range(chunks):
            values = v_refs[c][0, :, j * HEAD_SIZE : (j + 1) * HEAD_SIZE]
            terms = jnp.exp(score_ref[c] - highest)
            total = total + jnp.sum(terms, axis=-1, keepdims=True)
            mixed = mixed + multiply(terms.astype(jnp.bfloat16), values)
        outs += head_columns(mixed / total, length)
        totals += head_columns(highest + jnp.log(total), length)
    out_ref[...] = jnp.concatenate(outs, axis=1).astype(jnp.bfloat16)
    store_log_totals(lse_ref, totals)


def cross_backward_kernel(chunks, count_ref, base_ref, q_ref, g_ref, lse_ref, *refs):
    k_refs, v_refs = refs[:chunks], refs[chunks : 2 * chunks]
    dq_ref = refs[2 * chunks]
    d_refs = refs[2 * chunks + 1 : 3 * chunks + 1]
    probs_ref, product_ref = refs[3 * chunks + 1 :]
    length, rows = q_ref.shape[0], k_refs[0].shape[1]
    half = d_refs[0].shape[2] // 2
    count = count_ref[pl.program_id(0)]
    first = pl.program_id(1) * (PAIR * HEAD_SIZE)
    position = lax.broadcasted_iota(jnp.int32, (rows, 1), 0)
    dqs = []
    dks, dvs = [[] for _ in range(chunks)], [[] for _ in range(chunks)]
    for j in range(PAIR):
        queries = head_rows(q_ref, j)
        gradient = head_rows(g_ref, j)
        log_total = jnp.concatenate(
            [lse_ref[0, 0, j * SHARED + i : j * SHARED + i + 1, :] for i in range(SHARED)], axis=1
        )
        centre = 0.0
        for c in range(chunks):
            keys = k_refs[c][0, :, j * HEAD_SIZE : (j + 1) * HEAD_SIZE]
            values = v_refs[c][0, :, j * HEAD_SIZE : (j + 1) * HEAD_SIZE]
            scores = jnp.where(
                position + base_ref[c] < count, times_transposed(keys, queries), MASKED
            )
            probs = jnp.exp(scores - log_total)
            product = probs * times_transposed(values, gradient)
            centre = centre + jnp.sum(product, axis=0, keepdims=True)
            dvs[c].append(multiply(probs.astype(jnp.bfloat16), gradient))
            probs_ref[c] = probs
            product_ref[c] = product
        dq = 0.0
        for c in range(chunks):
            keys = k_refs[c][0, :, j * HEAD_SIZE : (j + 1) * HEAD_SIZE]
            score_grad = (product_ref[c] - probs_ref[c] * centre).astype(jnp.bfloat16)
            dks[c].append(multiply(score_grad, queries))
            dq = dq + outer_sum(keys, score_grad)
        dqs += head_columns(jnp.transpose(dq), length)
    dq_ref[...] = jnp.concatenate(dqs, axis=1).astype(jnp.bfloat16)
    for c in range(chunks):
        d_refs[c][0, :, pl.ds(pl.multiple_of(first, 128), 128)] = jnp.concatenate(
            dks[c], axis=1
        ).astype(jnp.bfloat16)
        d_refs[c][0, :, pl.ds(pl.multiple_of(half + first, 128), 128)] = jnp.concatenate(
            dvs[c], axis=1
        ).astype(jnp.bfloat16)


def feed_forward_kernel(
    n_ref, b_ref, wg_ref, wu_ref, wd_ref, hid_ref, gg_ref, gu_ref, y_ref, gn_ref
):
    root = float(np.sqrt(2.0 / np.pi))

    @pl.when(pl.program_id(0) == 0)
    def _():
        y_ref[...] = jnp.zeros_like(y_ref)
        gn_ref[...] = jnp.zeros_like(gn_ref)

    gate = multiply(n_ref[...], wg_ref[...])
    upward = multiply(n_ref[...], wu_ref[...])
    back = times_transposed(b_ref[...], wd_ref[...])
    square = gate * gate
    bend = jnp.tanh(root * gate * (1.0 + 0.044715 * square))
    half_sum = 0.5 * (1.0 + bend)
    activated = gate * half_sum
    slope = half_sum + 0.5 * gate * (1.0 - bend * bend) * (root * (1.0 + 3 * 0.044715 * square))
    hidden = (activated * upward).astype(jnp.bfloat16)
    grad_gate = (back * upward * slope).astype(jnp.bfloat16)
    grad_upward = (back * activated).astype(jnp.bfloat16)
    hid_ref[...] = hidden
    gg_ref[...] = grad_gate
    gu_ref[...] = grad_upward
    y_ref[...] += multiply(hidden, wd_ref[...])
    gn_ref[...] += times_transposed(grad_gate, wg_ref[...]) + times_transposed(
        grad_upward, wu_ref[...]
    )


def shape(dims, dtype):
    return jax.ShapeDtypeStruct(tuple(dims), dtype)


def self_attention(q, k, v, counts, base):
    seqs, length = counts.shape[0], q.shape[0] // counts.shape[0]
    wide, narrow = STEP_HEADS * HEAD_SIZE, PAIR * HEAD_SIZE
    return pl.pallas_call(
        self_forward_kernel,
        out_shape=(shape(q.shape, jnp.bfloat16), shape((seqs, PAIRS, 8, length), jnp.float32)),
        grid_spec=pltpu.PrefetchScalarGridSpec(
            num_scalar_prefetch=1,
            grid=(seqs, PAIRS),
            in_specs=[
                pl.BlockSpec((length, wide), lambda s, p, _: (s, p)),
                pl.BlockSpec((length, narrow), lambda s, p, _: (s, p)),
                pl.BlockSpec((length, narrow), lambda s, p, _: (s, p)),
                pl.BlockSpec((1, STEP_HEADS, length), lambda s, p, _: (p, 0, 0)),
            ],
            out_specs=(
                pl.BlockSpec((length, wide), lambda s, p, _: (s, p)),
                pl.BlockSpec((1, 1, 8, length), lambda s, p, _: (s, p, 0, 0)),
            ),
        ),
        name="self_forward",
    )(counts, q, k, v, base)


def self_attention_back(q, k, v, counts, base, lse, gradient):
    seqs, length = counts.shape[0], q.shape[0] // counts.shape[0]
    wide, narrow = STEP_HEADS * HEAD_SIZE, PAIR * HEAD_SIZE
    return pl.pallas_call(
        self_backward_kernel,
        out_shape=(
            shape(q.shape, jnp.bfloat16),
            shape(k.shape, jnp.bfloat16),
            shape(v.shape, jnp.bfloat16),
            shape((seqs, PAIRS, STEP_HEADS, length), jnp.float32),
        ),
        grid_spec=pltpu.PrefetchScalarGridSpec(
            num_scalar_prefetch=1,
            grid=(seqs, PAIRS),
            in_specs=[
                pl.BlockSpec((length, wide), lambda s, p, _: (s, p)),
                pl.BlockSpec((length, narrow), lambda s, p, _: (s, p)),
                pl.BlockSpec((length, narrow), lambda s, p, _: (s, p)),
                pl.BlockSpec((length, wide), lambda s, p, _: (s, p)),
                pl.BlockSpec((1, 1, 8, length), lambda s, p, _: (s, p, 0, 0)),
                pl.BlockSpec((1, STEP_HEADS, length), lambda s, p, _: (p, 0, 0)),
            ],
            out_specs=(
                pl.BlockSpec((length, wide), lambda s, p, _: (s, p)),
                pl.BlockSpec((length, narrow), lambda s, p, _: (s, p)),
                pl.BlockSpec((length, narrow), lambda s, p, _: (s, p)),
                pl.BlockSpec((1, 1, STEP_HEADS, length), lambda s, p, _: (s, p, 0, 0)),
            ),
        ),
        name="self_backward",
    )(counts, q, k, v, gradient, lse, base)


def chunk_specs(pieces):
    rows, narrow = pieces[0].shape[1], PAIR * HEAD_SIZE
    keys = [pl.BlockSpec((1, rows, narrow), lambda s, p, *_: (s, 0, p)) for _ in pieces]
    values = [pl.BlockSpec((1, rows, narrow), lambda s, p, *_: (s, 0, PAIRS + p)) for _ in pieces]
    return keys + values


def cross_attention(q, pieces, counts, bases):
    seqs, length, rows = counts.shape[0], q.shape[0] // counts.shape[0], pieces[0].shape[1]
    wide = STEP_HEADS * HEAD_SIZE
    return pl.pallas_call(
        functools.partial(cross_forward_kernel, len(pieces)),
        out_shape=(shape(q.shape, jnp.bfloat16), shape((seqs, PAIRS, 8, length), jnp.float32)),
        grid_spec=pltpu.PrefetchScalarGridSpec(
            num_scalar_prefetch=2,
            grid=(seqs, PAIRS),
            in_specs=[pl.BlockSpec((length, wide), lambda s, p, *_: (s, p))] + chunk_specs(pieces),
            out_specs=(
                pl.BlockSpec((length, wide), lambda s, p, *_: (s, p)),
                pl.BlockSpec((1, 1, 8, length), lambda s, p, *_: (s, p, 0, 0)),
            ),
            scratch_shapes=[pltpu.VMEM((len(pieces), SHARED * length, rows), jnp.float32)],
        ),
        name="cross_forward",
    )(counts, bases, q, *pieces, *pieces)


def cross_attention_back(q, pieces, counts, bases, lse, gradient):
    seqs, length, rows = counts.shape[0], q.shape[0] // counts.shape[0], pieces[0].shape[1]
    wide, chunks = STEP_HEADS * HEAD_SIZE, len(pieces)
    return pl.pallas_call(
        functools.partial(cross_backward_kernel, chunks),
        out_shape=(shape(q.shape, jnp.bfloat16),)
        + tuple(shape(piece.shape, jnp.bfloat16) for piece in pieces),
        grid_spec=pltpu.PrefetchScalarGridSpec(
            num_scalar_prefetch=2,
            grid=(seqs, PAIRS),
            in_specs=[
                pl.BlockSpec((length, wide), lambda s, p, *_: (s, p)),
                pl.BlockSpec((length, wide), lambda s, p, *_: (s, p)),
                pl.BlockSpec((1, 1, 8, length), lambda s, p, *_: (s, p, 0, 0)),
            ]
            + chunk_specs(pieces),
            out_specs=(pl.BlockSpec((length, wide), lambda s, p, *_: (s, p)),)
            + tuple(
                pl.BlockSpec((1,) + piece.shape[1:], lambda s, p, *_: (s, 0, 0)) for piece in pieces
            ),
            scratch_shapes=[pltpu.VMEM((chunks, rows, SHARED * length), jnp.float32)] * 2,
        ),
        name="cross_backward",
    )(counts, bases, q, gradient, lse, *pieces, *pieces)


def feed_forward(rows_normed, branch, w_gate, w_up, w_down):
    rows, width = rows_normed.shape
    hidden = w_gate.shape[1]
    tile = 256
    return pl.pallas_call(
        feed_forward_kernel,
        out_shape=(shape((rows, hidden), jnp.bfloat16),) * 3
        + (shape((rows, width), jnp.float32),) * 2,
        grid=(hidden // tile,),
        in_specs=[
            pl.BlockSpec((rows, width), lambda f: (0, 0)),
            pl.BlockSpec((rows, width), lambda f: (0, 0)),
            pl.BlockSpec((width, tile), lambda f: (0, f)),
            pl.BlockSpec((width, tile), lambda f: (0, f)),
            pl.BlockSpec((tile, width), lambda f: (f, 0)),
        ],
        out_specs=(pl.BlockSpec((rows, tile), lambda f: (0, f)),) * 3
        + (pl.BlockSpec((rows, width), lambda f: (0, 0)),) * 2,
        name="feed_forward",
    )(rows_normed, branch, w_gate, w_up, w_down)


def bit_count(size):
    return size.bit_length() - 1


def reduce_rows(term, order):
    devices, members = lax.axis_size("dp"), lax.axis_size("mem")
    me, member = lax.axis_index("dp"), lax.axis_index("mem")
    bits = bit_count(devices)
    rows, columns = term.shape
    share = rows // (devices * members)
    current = term.reshape((2,) * bits + (members, share, columns))
    left = list(range(bits - 1, -1, -1))
    for bit in order:
        axis = left.index(bit)
        left.remove(bit)
        mine = (me >> bit) & 1
        sent = lax.dynamic_index_in_dim(current, 1 - mine, axis, keepdims=False)
        got = lax.ppermute(sent, "dp", [(i, i ^ (1 << bit)) for i in range(devices)])
        kept = lax.dynamic_index_in_dim(current, mine, axis, keepdims=False)
        current = (kept.astype(jnp.float32) + got.astype(jnp.float32)).astype(jnp.bfloat16)
    total = lax.dynamic_index_in_dim(current, member, 0, keepdims=False).astype(jnp.float32)
    for sign in (1, -1):
        got = None
        for step in range(members - 1):
            place = member if sign == 1 else members - 1 - member
            block = jnp.clip(members - 1 - step + place, 0, members - 1)
            block = block if sign == 1 else members - 1 - block
            sent = lax.dynamic_index_in_dim(current, block, 0, keepdims=False)
            if got is not None:
                sent = (sent.astype(jnp.float32) + got.astype(jnp.float32)).astype(jnp.bfloat16)
            pairs = [(i, i + 1) for i in range(step + 1)]
            if sign == -1:
                pairs = [(members - 1 - a, members - 1 - b) for a, b in pairs]
            got = lax.ppermute(sent, "mem", pairs)
        total = total + got.astype(jnp.float32)
    return total


LANES = 128


def partner_masks(order):
    stages = len(order)
    masks = []
    for place in range(1 << stages):
        mask = 0
        for stage, bit in enumerate(order):
            if not (place >> (stages - 1 - stage)) & 1:
                mask |= 1 << bit
        masks.append(mask)
    return masks


def outer_kernel(lefts, chunk, segments, orders, me_ref, *refs):
    a_refs, refs = refs[:lefts], refs[lefts:]
    b_refs, refs = refs[: lefts * len(segments)], refs[lefts * len(segments) :]
    outs, refs = refs[: 2 * len(orders)], refs[2 * len(orders) :]
    plain_ref, arranged = refs[0], refs[1:]
    blocks = 1 << len(orders[0])
    block = plain_ref.shape[0] // blocks
    members, share = outs[0].shape[1], outs[0].shape[2] // chunk
    me = me_ref[0]

    @pl.when(pl.program_id(0) == 0)
    def _():
        tokens = a_refs[0].shape[0]
        for index, a_ref in enumerate(a_refs):
            plain_ref[:, index * tokens : (index + 1) * tokens] = jnp.transpose(a_ref[...])
        for order, arranged_ref in zip(orders, arranged):
            for place, mask in enumerate(partner_masks(order)):
                source = pl.multiple_of((me ^ mask) * block, 16)
                arranged_ref[place * block : (place + 1) * block] = plain_ref[
                    pl.ds(source, block)
                ]

    step = 0
    for index, (steps, color) in enumerate(segments):
        rights = b_refs[lefts * index : lefts * (index + 1)]

        @pl.when((pl.program_id(0) >= step) & (pl.program_id(0) < step + steps))
        def _(color=color, rights=rights):
            right = joined([right_ref[...] for right_ref in rights], 0)
            product = multiply(arranged[color][...], right).astype(jnp.bfloat16)
            for place in range(blocks):
                half_ref = outs[2 * color + (0 if place < blocks // 2 else 1)]
                for m in range(members):
                    first = place * block + m * share
                    for tile in range(chunk):
                        half_ref[place % (blocks // 2), m, tile * share : (tile + 1) * share] = (
                            product[first : first + share, tile * LANES : (tile + 1) * LANES]
                        )

        step += steps


def outer_arranged(lefts, parts, orders, chunk):
    tokens, features = lefts[0].shape
    devices, members = lax.axis_size("dp"), lax.axis_size("mem")
    share = features // (devices * members)
    half = devices // 2
    wide = chunk * LANES
    segments, in_specs, operands, step = [], [], [], 0
    totals = [0] * len(orders)
    for rights, first, columns, color in parts:
        steps = columns // wide
        segments.append((steps, color))
        totals[color] += steps
        for right in rights:
            operands.append(right)
            in_specs.append(
                pl.BlockSpec(
                    (tokens, wide),
                    lambda j, _, step=step, steps=steps, first=first: (
                        0,
                        first // wide + jnp.clip(j - step, 0, steps - 1),
                    ),
                )
            )
        step += steps
    out_shape, out_specs, before = [], [], 0
    for total in totals:
        for _ in range(2):
            out_shape.append(shape((half, members, share * chunk * total, LANES), jnp.bfloat16))
            out_specs.append(
                pl.BlockSpec(
                    (half, members, share * chunk, LANES),
                    lambda j, _, before=before, total=total: (
                        0,
                        0,
                        jnp.clip(j - before, 0, total - 1),
                        0,
                    ),
                )
            )
        before += total
    me = lax.axis_index("dp").astype(jnp.int32).reshape(1)
    kernel = functools.partial(
        outer_kernel, len(lefts), chunk, tuple(segments), tuple(tuple(o) for o in orders)
    )
    return pl.pallas_call(
        kernel,
        out_shape=tuple(out_shape),
        grid_spec=pltpu.PrefetchScalarGridSpec(
            num_scalar_prefetch=1,
            grid=(step,),
            in_specs=[pl.BlockSpec((tokens, features), lambda j, _: (0, 0))] * len(lefts) + in_specs,
            out_specs=tuple(out_specs),
            scratch_shapes=[pltpu.VMEM((features, tokens * len(lefts)), jnp.bfloat16)]
            * (1 + len(orders)),
        ),
        name="outer",
    )(me, *lefts, *operands)


def project_kernel(members, place_ref, x_ref, ck_ref, cv_ref, *out_refs):
    width = ck_ref.shape[1]
    for index in range(members):

        @pl.when(pl.program_id(0) == index)
        def _(index=index):
            out_ref = out_refs[index]
            rows = x_ref[0].reshape(-1, x_ref.shape[-1])
            kept = out_ref.shape[:2] + (width,)
            out_ref[:, :, :width] = (
                multiply(rows, ck_ref[...]).astype(jnp.bfloat16).reshape(kept)
            )
            out_ref[:, :, width:] = (
                multiply(rows, cv_ref[...]).astype(jnp.bfloat16).reshape(kept)
            )


def project_memory(memory, m, seqs, c_key, c_value):
    members = lax.axis_size("mem")
    _, _, rows, width = memory.shape
    kept = (seqs, rows, c_key.shape[1] + c_value.shape[1])
    me = lax.axis_index("mem").astype(jnp.int32).reshape(1)
    found = pl.pallas_call(
        functools.partial(project_kernel, members),
        out_shape=(shape(kept, jnp.bfloat16),) * members,
        grid_spec=pltpu.PrefetchScalarGridSpec(
            num_scalar_prefetch=1,
            grid=(members,),
            in_specs=[
                pl.BlockSpec(
                    (1, seqs, rows, width),
                    lambda t, me: (m, lax.rem(me[0] + t + 1, members), 0, 0),
                ),
                pl.BlockSpec(c_key.shape, lambda t, _: (0, 0)),
                pl.BlockSpec(c_value.shape, lambda t, _: (0, 0)),
            ],
            out_specs=(pl.BlockSpec(kept, lambda t, _: (0, 0, 0)),) * members,
        ),
        name="project",
    )(me, memory, c_key, c_value)
    return [found[-1]] + list(found[:-1])


def memory_kernel(pieces, orders, place_ref, x_ref, ck_ref, cv_ref, *refs):
    piece_refs, refs = refs[:pieces], refs[pieces:]
    grad_ref, outs, (now_ref, sum_ref) = refs[0], refs[1:5], refs[5:]
    step, width = pl.program_id(0), ck_ref.shape[1]

    @pl.when(step == 0)
    def _():
        sum_ref[...] = jnp.zeros_like(sum_ref)

    for index in range(pieces):

        @pl.when(step == index)
        def _(index=index):
            now_ref[...] = piece_refs[index][...].reshape(now_ref.shape)

    now = now_ref[...]
    grad = times_transposed(now[:, :width], ck_ref[...]) + times_transposed(
        now[:, width:], cv_ref[...]
    )
    grad_ref[0] = grad.astype(jnp.bfloat16).reshape(grad_ref.shape[1:])
    sum_ref[...] += outer_sum(x_ref[0].reshape(-1, x_ref.shape[-1]), now)

    @pl.when(step == pieces - 1)
    def _():
        blocks = 1 << len(orders[0])
        block = sum_ref.shape[0] // blocks
        members = outs[0].shape[1]
        tiles = width // LANES
        share = block // members
        for color, order in enumerate(orders):
            for place, mask in enumerate(partner_masks(order)):
                source = pl.multiple_of((place_ref[0] ^ mask) * block, 8)
                half_ref = outs[2 * color + (0 if place < blocks // 2 else 1)]
                found = sum_ref[pl.ds(source, block), color * width : (color + 1) * width]
                found = found.astype(jnp.bfloat16)
                for m in range(members):
                    for tile in range(tiles):
                        half_ref[place % (blocks // 2), m, tile * share : (tile + 1) * share] = (
                            found[m * share : (m + 1) * share, tile * LANES : (tile + 1) * LANES]
                        )


def memory_backward(memory, pieces, c_key, c_value, orders):
    devices, members = lax.axis_size("dp"), lax.axis_size("mem")
    seqs, rows, both = pieces[0].shape
    width = memory.shape[-1]
    half, share = devices // 2, width // (devices * members)
    kept = (half, members, share * (both // 2 // LANES), LANES)
    place = jnp.stack([lax.axis_index("dp"), lax.axis_index("mem")]).astype(jnp.int32)

    def block_index(t, place):
        return (t // members, lax.rem(place[1] + lax.rem(t, members), members), 0, 0)

    found = pl.pallas_call(
        functools.partial(memory_kernel, len(pieces), tuple(tuple(o) for o in orders)),
        out_shape=(shape(memory.shape, jnp.bfloat16),) + (shape(kept, jnp.bfloat16),) * 4,
        grid_spec=pltpu.PrefetchScalarGridSpec(
            num_scalar_prefetch=1,
            grid=(len(pieces),),
            in_specs=[
                pl.BlockSpec((1, seqs, rows, width), block_index),
                pl.BlockSpec(c_key.shape, lambda t, _: (0, 0)),
                pl.BlockSpec(c_value.shape, lambda t, _: (0, 0)),
            ]
            + [pl.BlockSpec((seqs, rows, both), lambda t, _: (0, 0, 0))] * len(pieces),
            out_specs=(pl.BlockSpec((1, seqs, rows, width), block_index),)
            + (pl.BlockSpec(kept, lambda t, _: (0, 0, 0, 0)),) * 4,
            scratch_shapes=[
                pltpu.VMEM((seqs * rows, both), jnp.bfloat16),
                pltpu.VMEM((width, both), jnp.float32),
            ],
        ),
        name="memory_backward",
    )(place, memory, c_key, c_value, *pieces)
    return found[0], found[1:3], found[3:5]


def swap(array, bit):
    size = lax.axis_size("dp")
    return lax.ppermute(array, "dp", [(i, i ^ (1 << bit)) for i in range(size)])


def add16(left, right):
    return (left.astype(jnp.float32) + right.astype(jnp.float32)).astype(jnp.bfloat16)


def joined(arrays, axis):
    return arrays[0] if len(arrays) == 1 else jnp.concatenate(arrays, axis=axis)


def first_swap(pairs, bit):
    return [(swap(sent, bit), kept) for sent, kept in pairs]


def halves_of(pairs):
    half = pairs[0][0].shape[0] // 2
    sent = joined([add16(kept[:half], got[:half]) for got, kept in pairs], 2)
    kept = joined([add16(kept[half:], got[half:]) for got, kept in pairs], 2)
    return sent, kept


def next_stage(pairs, bit):
    sent, kept = halves_of(pairs)
    return [(swap(sent, bit), kept)]


def later_stages(pairs, bits):
    for bit in bits:
        pairs = next_stage(pairs, bit)
    return pairs


def whole_of(pairs):
    return joined([add16(kept, got) for got, kept in pairs], 2)[0]


def along_members(current):
    members, member = lax.axis_size("mem"), lax.axis_index("mem")
    total = lax.dynamic_index_in_dim(current, member, 0, keepdims=False).astype(jnp.float32)
    got = [None, None]
    for step in range(members - 1):
        for side in range(2):
            place = member if side == 0 else members - 1 - member
            block = jnp.clip(members - 1 - step + place, 0, members - 1)
            block = block if side == 0 else members - 1 - block
            sent = lax.dynamic_index_in_dim(current, block, 0, keepdims=False)
            if step:
                sent = add16(sent, got[side])
            pairs = [(i, i + 1) for i in range(step + 1)]
            if side == 1:
                pairs = [(members - 1 - a, members - 1 - b) for a, b in pairs]
            got[side] = lax.ppermute(sent, "mem", pairs)
    return total + got[0].astype(jnp.float32) + got[1].astype(jnp.float32)


def members_sum(pairs):
    flat = [item for pair in pairs for item in pair if item is not None]
    ends = np.cumsum([0] + [item.shape[1] for item in flat])
    total = along_members(jnp.concatenate(flat, axis=1))
    parts = iter([total[ends[i] : ends[i + 1]] for i in range(len(flat))])
    return [tuple(None if item is None else next(parts) for item in pair) for pair in pairs]


def rows_out(total, share, columns, first):
    tiles = columns // LANES
    part = total[first : first + share * tiles].reshape(tiles, share, LANES)
    return part.transpose(1, 0, 2).reshape(share, columns)


def sum_everywhere(value):
    for axis in ("mem", "dp"):
        size = lax.axis_size(axis)
        for bit in range(bit_count(size)):
            value = value + lax.ppermute(value, axis, [(i, i ^ (1 << bit)) for i in range(size)])
    return value


def per_device(
    target_in,
    memory,
    target_len,
    mem_len,
    cotangent,
    gain_self,
    gain_cross,
    gain_ffn,
    rel_table,
    w_query,
    w_key,
    w_value,
    w_out,
    c_query,
    c_key,
    c_value,
    c_out,
    w_gate,
    w_up,
    w_down,
):
    micro, seqs, length, width = target_in.shape
    mem_rows = memory.shape[2]
    members, member = lax.axis_size("mem"), lax.axis_index("mem")
    devices = lax.axis_size("dp")
    bits = bit_count(devices)
    order_a = list(range(bits))
    order_b = [0] + order_a[:0:-1]
    orders = (order_a, order_b)
    count, rows = micro * seqs, seqs * length
    key_width, hidden_width = c_key.shape[1], w_gate.shape[1]
    share, share_down = width // (devices * members), hidden_width // (devices * members)
    half = width // 2
    steps = range(micro)

    def shifted(array, shift):
        return lax.ppermute(array, "mem", [(i, (i + shift) % members) for i in range(members)])

    pieces = []
    for m in steps:
        found = project_memory(memory, m, seqs, c_key, c_value)
        pieces.append([found[0]] + [shifted(found[i], i) for i in range(1, members)])
    bases = jnp.stack(
        [lax.rem(member + members - shift, members) * mem_rows for shift in range(members)]
    ).astype(jnp.int32)

    target_counts = target_len.reshape(count)
    onehot = bucket_onehot(length)
    backwards = onehot[:, (-np.arange(length)) % length]
    base = jnp.dot(rel_table.T, jnp.asarray(onehot), precision=EXACT_PRECISION)
    base = base.reshape(PAIRS, STEP_HEADS, length)
    base_back = jnp.dot(rel_table.T, jnp.asarray(backwards), precision=EXACT_PRECISION)
    base_back = base_back.reshape(PAIRS, STEP_HEADS, length)

    inputs = target_in.reshape(count * length, width).astype(jnp.float32)
    normed_self = normed(inputs, gain_self)
    queries = multiply(normed_self, w_query).astype(jnp.bfloat16)
    keys = multiply(normed_self, w_key).astype(jnp.bfloat16)
    values = multiply(normed_self, w_value).astype(jnp.bfloat16)
    attended, self_lse = self_attention(queries, keys, values, target_counts, base_back)

    position = jnp.arange(length)
    outs, after_selfs, normed_crosses, cross_queries_all, mixed_all = [], [], [], [], []
    normed_ffns, branches_ffn, hiddens, gates, ups = [], [], [], [], []
    branches_cross, grad_queries_cross, branches_self = [], [], []
    grad_after_selfs, grads_attended = [], []
    sum_gain_ffn = sum_gain_cross = 0.0
    for m in steps:
        after_self = inputs[m * rows : (m + 1) * rows] + multiply(
            attended[m * rows : (m + 1) * rows], w_out
        )
        after_selfs.append(after_self)
        normed_crosses.append(normed(after_self, gain_cross))
        cross_queries_all.append(multiply(normed_crosses[m], c_query).astype(jnp.bfloat16))
    grad_pieces = []
    for m in steps:
        after_self, cross_queries = after_selfs[m], cross_queries_all[m]
        memory_counts = mem_len[m]
        cross_mixed, cross_lse = cross_attention(cross_queries, pieces[m], memory_counts, bases)
        mixed_all.append(cross_mixed)
        after_cross = after_self + multiply(cross_mixed, c_out)
        normed_ffn = normed(after_cross, gain_ffn)
        normed_ffns.append(normed_ffn)
        valid = (position[None, :] < target_len[m][:, None]).reshape(rows, 1)
        branch_ffn = jnp.where(valid, cotangent[m].reshape(rows, width), 0)
        branches_ffn.append(branch_ffn)
        grad_result = branch_ffn.astype(jnp.float32)
        hidden, grad_gate, grad_upward, ffn_out, grad_normed = feed_forward(
            normed_ffn, branch_ffn, w_gate, w_up, w_down
        )
        hiddens.append(hidden)
        gates.append(grad_gate)
        ups.append(grad_upward)
        outs.append(jnp.where(valid, after_cross + ffn_out, 0.0).astype(jnp.bfloat16))
        if m == micro - 1:
            gate_pairs = []
            for rights, order in ((gates, order_a), (ups, order_b)):
                found = outer_arranged(
                    normed_ffns,
                    [(rights, 0, hidden_width, 0)],
                    (order,),
                    hidden_width // (2 * LANES),
                )
                found = first_swap([found], 0)
                gate_pairs.append(next_stage(found, order[1]))
            packed_down = share_down % 8 == 0 and (hidden_width // devices) % 16 == 0
            if packed_down:
                found = outer_arranged(
                    hiddens,
                    [(branches_ffn, 0, half, 0), (branches_ffn, half, half, 1)],
                    orders,
                    half // LANES,
                )
                down_pairs = first_swap([found[0:2]], 0), first_swap([found[2:4]], 0)
                down_pairs = [
                    next_stage(pairs, order[1]) for pairs, order in zip(down_pairs, orders)
                ]
        part, gain_part = norm_back(after_cross, gain_ffn, grad_normed)
        sum_gain_ffn = sum_gain_ffn + gain_part
        grad_after_cross = grad_result + part
        branch_cross = grad_after_cross.astype(jnp.bfloat16)
        branches_cross.append(branch_cross)
        grad_cross_mixed = times_transposed(branch_cross, c_out).astype(jnp.bfloat16)
        found = cross_attention_back(
            cross_queries, pieces[m], memory_counts, bases, cross_lse, grad_cross_mixed
        )
        grad_queries_cross.append(found[0])
        for shift in range(members):
            piece = found[1 + shift]
            if shift:
                piece = shifted(piece, members - shift)
            grad_pieces.append(piece)
        part, gain_part = norm_back(
            after_self, gain_cross, times_transposed(found[0], c_query)
        )
        sum_gain_cross = sum_gain_cross + gain_part
        grad_after_self = grad_after_cross + part
        grad_after_selfs.append(grad_after_self)
        branches_self.append(grad_after_self.astype(jnp.bfloat16))
        grads_attended.append(times_transposed(branches_self[m], w_out).astype(jnp.bfloat16))
    chunk = key_width // LANES
    c_out_sum = outer_arranged(mixed_all, [(branches_cross, 0, width, 0)], (order_a,), chunk)
    c_query_sum = outer_arranged(
        normed_crosses, [(grad_queries_cross, 0, width, 0)], (order_b,), chunk
    )
    attended_parts = [attended[m * rows : (m + 1) * rows] for m in steps]
    w_out_sum = outer_arranged(
        attended_parts,
        [(branches_self, 0, half, 0), (branches_self, half, half, 1)],
        orders,
        chunk,
    )
    rest_pairs = (
        first_swap([c_out_sum, w_out_sum[0:2]], 0),
        first_swap([c_query_sum, w_out_sum[2:4]], 0),
    )
    ffn = [[whole_of(later_stages(p, o[2:])) for p, o in zip(gate_pairs, orders)]]
    if packed_down:
        ffn.append([whole_of(later_stages(p, o[2:])) for p, o in zip(down_pairs, orders)])
    rest_pairs = [next_stage(p, o[1]) for p, o in zip(rest_pairs, orders)]
    rest_a, rest_b = [whole_of(later_stages(p, o[2:])) for p, o in zip(rest_pairs, orders)]

    grad_queries, grad_keys, grad_values, diagonals = self_attention_back(
        queries,
        keys,
        values,
        target_counts,
        base,
        self_lse,
        jnp.concatenate(grads_attended, axis=0),
    )
    w_self_sum = outer_arranged(
        [normed_self],
        [
            ([grad_keys], 0, key_width, 0),
            ([grad_queries], 0, width, 1),
            ([grad_values], 0, key_width, 1),
        ],
        orders,
        chunk,
    )
    self_pairs = first_swap([w_self_sum[0:2]], 0), first_swap([w_self_sum[2:4]], 0)
    self_pairs = [next_stage(p, o[1]) for p, o in zip(self_pairs, orders)]
    self_a, self_b = [whole_of(later_stages(p, o[2:])) for p, o in zip(self_pairs, orders)]
    (gate_a, gate_b), (down_a, down_b) = members_sum(ffn + [(None, None)] * (2 - len(ffn)))
    g_gate = rows_out(gate_a, share, hidden_width, 0)
    g_up = rows_out(gate_b, share, hidden_width, 0)
    if packed_down:
        g_down = jnp.concatenate(
            [rows_out(part, share_down, half, 0) for part in (down_a, down_b)], axis=1
        )
    else:
        g_down = reduce_rows(
            outer_sum(jnp.concatenate(hiddens), jnp.concatenate(branches_ffn)).astype(jnp.bfloat16),
            order_a,
        )

    grad_normed = (
        times_transposed(grad_queries, w_query)
        + times_transposed(grad_keys, w_key)
        + times_transposed(grad_values, w_value)
    )
    part, sum_gain_self = norm_back(inputs, gain_self, grad_normed)
    target_grad = (jnp.concatenate(grad_after_selfs, axis=0) + part).astype(jnp.bfloat16)
    distances = jnp.sum(diagonals, axis=0).reshape(QUERY_HEADS, length)
    table = jnp.dot(distances, jnp.asarray(onehot.T), precision=EXACT_PRECISION).T

    memory_grad, memory_a, memory_b = memory_backward(memory, grad_pieces, c_key, c_value, orders)
    pairs_a = first_swap([memory_a], 0)
    pairs_b = first_swap([memory_b], 0)
    memory_a = whole_of(later_stages(pairs_a, order_a[1:]))
    memory_b = whole_of(later_stages(pairs_b, order_b[1:]))
    (rest_a, rest_b), (self_a, self_b), (memory_a, memory_b) = members_sum(
        [(rest_a, rest_b), (self_a, self_b), (memory_a, memory_b)]
    )
    tile_rows = share * (width // LANES)
    g_c_out = rows_out(rest_a, share, width, 0)
    g_c_query = rows_out(rest_b, share, width, 0)
    g_w_out = jnp.concatenate(
        [rows_out(part, share, half, tile_rows) for part in (rest_a, rest_b)], axis=1
    )
    g_w_key = rows_out(self_a, share, key_width, 0)
    g_w_query = rows_out(self_b, share, width, 0)
    g_w_value = rows_out(self_b, share, key_width, tile_rows)
    g_c_key = rows_out(memory_a, share, key_width, 0)
    g_c_value = rows_out(memory_b, share, key_width, 0)

    small = sum_everywhere(
        jnp.concatenate([sum_gain_self, sum_gain_cross, sum_gain_ffn, table.reshape(-1)])
    )
    return (
        jnp.stack(outs).reshape(micro, seqs, length, width),
        target_grad.reshape(micro, seqs, length, width),
        memory_grad,
        small[:width],
        small[width : 2 * width],
        small[2 * width : 3 * width],
        small[3 * width :].reshape(NB, QUERY_HEADS),
        g_w_query,
        g_w_key,
        g_w_value,
        g_w_out,
        g_c_query,
        g_c_key,
        g_c_value,
        g_c_out,
        g_gate,
        g_up,
        g_down,
    )


def solution(mesh):
    rows = P(None, ("dp", "mem"), None, None)
    lengths = P(None, ("dp", "mem"))
    encoded = P(None, "dp", "mem", None)
    return jax.shard_map(
        per_device,
        mesh=mesh,
        in_specs=(rows, encoded, lengths, lengths, rows) + (P(),) * 15,
        out_specs=(rows, rows, encoded) + (P(),) * 4 + (P(("dp", "mem"), None),) * 11,
        check_vma=False,
    )
```

```python
import functools

import jax
import jax.numpy as jnp
import numpy as np
from jax import lax
from jax.experimental import pallas as pl
from jax.experimental.pallas import tpu as pltpu
from jax.sharding import PartitionSpec as P


QUERY_HEADS = 16
HEAD_SIZE = 64
KEY_VALUE_HEADS = 8
NB = 32
MAXD = 128
SHARED = QUERY_HEADS // KEY_VALUE_HEADS
PAIR = 2
PAIRS = KEY_VALUE_HEADS // PAIR
STEP_HEADS = PAIR * SHARED

EPSILON = 1e-06
MASKED = -1e30
EXACT_PRECISION = lax.Precision.HIGHEST


def bucket_index(length):
    half = NB // 2
    distance = np.arange(length)
    spread = np.floor(np.log(np.maximum(distance, half) / half) / np.log(MAXD / half) * half)
    return np.where(distance < half, distance, np.minimum(spread + half, NB - 1)).astype(np.int64)


def bucket_onehot(length):
    chosen = bucket_index(length)
    return np.where(chosen[None, :] == np.arange(NB)[:, None], 1.0, 0.0).astype(np.float32)


def inverse_rms(rows):
    return lax.rsqrt(jnp.mean(rows * rows, axis=-1, keepdims=True) + EPSILON)


def normed(rows, gain):
    return (rows * inverse_rms(rows) * gain).astype(jnp.bfloat16)


def norm_back(rows, gain, gradient):
    scale = inverse_rms(rows)
    scaled = gradient * gain
    shared = jnp.mean(scaled * rows, axis=-1, keepdims=True)
    part_rows = scale * scaled - rows * (scale * scale * scale * shared)
    return part_rows, jnp.sum(gradient * rows * scale, axis=0)


def dot32(left, right, dims):
    return lax.dot_general(left, right, (dims, ((), ())), preferred_element_type=jnp.float32)


def multiply(left, right):
    return dot32(left, right, ((1,), (0,)))


def outer_sum(left, right):
    return dot32(left, right, ((0,), (0,)))


def times_transposed(left, right):
    return dot32(left, right, ((1,), (1,)))


def head_rows(ref_rows, key_head):
    first = key_head * SHARED * HEAD_SIZE
    return jnp.concatenate(
        [ref_rows[:, first + i * HEAD_SIZE : first + (i + 1) * HEAD_SIZE] for i in range(SHARED)],
        axis=0,
    )


def head_columns(rows, length):
    return [rows[i * length : (i + 1) * length] for i in range(SHARED)]


def store_log_totals(lse_ref, columns):
    length = columns[0].shape[0]
    lane = lax.broadcasted_iota(jnp.int32, (length, 128), 1)
    packed = jnp.zeros((length, 128), jnp.float32)
    for index, column in enumerate(columns):
        packed = jnp.where(lane == index, column, packed)
    lse_ref[0, 0] = jnp.transpose(packed)[:8]


def self_forward_kernel(count_ref, q_ref, k_ref, v_ref, base_ref, out_ref, lse_ref):
    length = q_ref.shape[0]
    count = count_ref[pl.program_id(0)]
    row = lax.broadcasted_iota(jnp.int32, (length, length), 0)
    column = lax.broadcasted_iota(jnp.int32, (length, length), 1)
    keep = (column <= row) & (column < count)
    keep = jnp.concatenate([keep.astype(jnp.float32)] * SHARED, axis=0) > 0.5
    outs, totals = [], []
    for j in range(PAIR):
        queries = head_rows(q_ref, j)
        keys = k_ref[:, j * HEAD_SIZE : (j + 1) * HEAD_SIZE]
        values = v_ref[:, j * HEAD_SIZE : (j + 1) * HEAD_SIZE]
        bias = jnp.concatenate(
            [
                pltpu.roll(
                    jnp.broadcast_to(base_ref[0, j * SHARED + i : j * SHARED + i + 1, :], (length, length)),
                    0,
                    1,
                    stride=1,
                    stride_axis=0,
                )
                for i in range(SHARED)
            ],
            axis=0,
        )
        scores = jnp.where(keep, times_transposed(queries, keys) + bias, MASKED)
        highest = jnp.max(scores, axis=-1, keepdims=True)
        terms = jnp.exp(scores - highest)
        total = jnp.sum(terms, axis=-1, keepdims=True)
        mixed = multiply(terms.astype(jnp.bfloat16), values) / total
        outs += head_columns(mixed, length)
        totals += head_columns(highest + jnp.log(total), length)
    out_ref[...] = jnp.concatenate(outs, axis=1).astype(jnp.bfloat16)
    store_log_totals(lse_ref, totals)


def diagonal_sums(square):
    length = square.shape[0]
    group = 8
    total = square[:group]
    for first in range(group, length, group):
        total = total + pltpu.roll(square[first : first + group], length - first, 1)
    row = lax.broadcasted_iota(jnp.int32, (group, length), 0)
    sums = jnp.where(row == 0, total, 0.0)
    for r in range(1, group):
        sums = sums + jnp.where(row == r, pltpu.roll(total, length - r, 1), 0.0)
    return jnp.sum(sums, axis=0, keepdims=True)


def self_backward_kernel(
    count_ref, q_ref, k_ref, v_ref, g_ref, lse_ref, base_ref, dq_ref, dk_ref, dv_ref, diag_ref
):
    length = q_ref.shape[0]
    count = count_ref[pl.program_id(0)]
    row = lax.broadcasted_iota(jnp.int32, (length, length), 0)
    column = lax.broadcasted_iota(jnp.int32, (length, length), 1)
    keep = (row <= column) & (row < count)
    dqs, dks, dvs, diagonals = [], [], [], []
    for j in range(PAIR):
        queries = head_rows(q_ref, j)
        gradient = head_rows(g_ref, j)
        keys = k_ref[:, j * HEAD_SIZE : (j + 1) * HEAD_SIZE]
        values = v_ref[:, j * HEAD_SIZE : (j + 1) * HEAD_SIZE]
        scores_all = times_transposed(keys, queries)
        grad_all = times_transposed(values, gradient)
        weights, score_grads = [], []
        for i in range(SHARED):
            h = j * SHARED + i
            bias = pltpu.roll(
                jnp.broadcast_to(base_ref[0, h : h + 1, :], (length, length)),
                0,
                1,
                stride=1,
                stride_axis=0,
            )
            scores = scores_all[:, i * length : (i + 1) * length] + bias
            scores = jnp.where(keep, scores, MASKED)
            probs = jnp.exp(scores - lse_ref[0, 0, h : h + 1, :])
            weights.append(probs.astype(jnp.bfloat16))
            product = probs * grad_all[:, i * length : (i + 1) * length]
            centre = jnp.sum(product, axis=0, keepdims=True)
            score_grad = (product - probs * centre).astype(jnp.bfloat16)
            score_grads.append(score_grad)
            diagonals.append(diagonal_sums(score_grad.astype(jnp.float32)))
        weights = jnp.concatenate(weights, axis=1)
        score_grads = jnp.concatenate(score_grads, axis=1)
        dvs.append(multiply(weights, gradient))
        dks.append(multiply(score_grads, queries))
        dq = jnp.transpose(outer_sum(keys, score_grads))
        dqs += head_columns(dq, length)
    dq_ref[...] = jnp.concatenate(dqs, axis=1).astype(jnp.bfloat16)
    dk_ref[...] = jnp.concatenate(dks, axis=1).astype(jnp.bfloat16)
    dv_ref[...] = jnp.concatenate(dvs, axis=1).astype(jnp.bfloat16)
    diag_ref[0, 0] = jnp.concatenate(diagonals, axis=0)


def cross_forward_kernel(chunks, count_ref, base_ref, q_ref, *refs):
    k_refs, v_refs = refs[:chunks], refs[chunks : 2 * chunks]
    out_ref, lse_ref, score_ref = refs[2 * chunks :]
    length, rows = q_ref.shape[0], k_refs[0].shape[1]
    count = count_ref[pl.program_id(0)]
    column = lax.broadcasted_iota(jnp.int32, (1, rows), 1)
    outs, totals = [], []
    for j in range(PAIR):
        queries = head_rows(q_ref, j)
        highest = None
        for c in range(chunks):
            keys = k_refs[c][0, :, j * HEAD_SIZE : (j + 1) * HEAD_SIZE]
            scores = jnp.where(
                column + base_ref[c] < count, times_transposed(queries, keys), MASKED
            )
            score_ref[c] = scores
            top = jnp.max(scores, axis=-1, keepdims=True)
            highest = top if highest is None else jnp.maximum(highest, top)
        total, mixed = 0.0, 0.0
        for c in range(chunks):
            values = v_refs[c][0, :, j * HEAD_SIZE : (j + 1) * HEAD_SIZE]
            terms = jnp.exp(score_ref[c] - highest)
            total = total + jnp.sum(terms, axis=-1, keepdims=True)
            mixed = mixed + multiply(terms.astype(jnp.bfloat16), values)
        outs += head_columns(mixed / total, length)
        totals += head_columns(highest + jnp.log(total), length)
    out_ref[...] = jnp.concatenate(outs, axis=1).astype(jnp.bfloat16)
    store_log_totals(lse_ref, totals)


def cross_backward_kernel(chunks, count_ref, base_ref, q_ref, g_ref, lse_ref, *refs):
    k_refs, v_refs = refs[:chunks], refs[chunks : 2 * chunks]
    dq_ref = refs[2 * chunks]
    d_refs = refs[2 * chunks + 1 : 3 * chunks + 1]
    probs_ref, product_ref = refs[3 * chunks + 1 :]
    length, rows = q_ref.shape[0], k_refs[0].shape[1]
    half = d_refs[0].shape[2] // 2
    count = count_ref[pl.program_id(0)]
    first = pl.program_id(1) * (PAIR * HEAD_SIZE)
    position = lax.broadcasted_iota(jnp.int32, (rows, 1), 0)
    dqs = []
    dks, dvs = [[] for _ in range(chunks)], [[] for _ in range(chunks)]
    for j in range(PAIR):
        queries = head_rows(q_ref, j)
        gradient = head_rows(g_ref, j)
        log_total = jnp.concatenate(
            [lse_ref[0, 0, j * SHARED + i : j * SHARED + i + 1, :] for i in range(SHARED)], axis=1
        )
        centre = 0.0
        for c in range(chunks):
            keys = k_refs[c][0, :, j * HEAD_SIZE : (j + 1) * HEAD_SIZE]
            values = v_refs[c][0, :, j * HEAD_SIZE : (j + 1) * HEAD_SIZE]
            scores = jnp.where(
                position + base_ref[c] < count, times_transposed(keys, queries), MASKED
            )
            probs = jnp.exp(scores - log_total)
            product = probs * times_transposed(values, gradient)
            centre = centre + jnp.sum(product, axis=0, keepdims=True)
            dvs[c].append(multiply(probs.astype(jnp.bfloat16), gradient))
            probs_ref[c] = probs
            product_ref[c] = product
        dq = 0.0
        for c in range(chunks):
            keys = k_refs[c][0, :, j * HEAD_SIZE : (j + 1) * HEAD_SIZE]
            score_grad = (product_ref[c] - probs_ref[c] * centre).astype(jnp.bfloat16)
            dks[c].append(multiply(score_grad, queries))
            dq = dq + outer_sum(keys, score_grad)
        dqs += head_columns(jnp.transpose(dq), length)
    dq_ref[...] = jnp.concatenate(dqs, axis=1).astype(jnp.bfloat16)
    for c in range(chunks):
        d_refs[c][0, :, pl.ds(pl.multiple_of(first, 128), 128)] = jnp.concatenate(
            dks[c], axis=1
        ).astype(jnp.bfloat16)
        d_refs[c][0, :, pl.ds(pl.multiple_of(half + first, 128), 128)] = jnp.concatenate(
            dvs[c], axis=1
        ).astype(jnp.bfloat16)


def feed_forward_kernel(
    n_ref, b_ref, wg_ref, wu_ref, wd_ref, hid_ref, gg_ref, gu_ref, y_ref, gn_ref
):
    root = float(np.sqrt(2.0 / np.pi))

    @pl.when(pl.program_id(0) == 0)
    def _():
        y_ref[...] = jnp.zeros_like(y_ref)
        gn_ref[...] = jnp.zeros_like(gn_ref)

    gate = multiply(n_ref[...], wg_ref[...])
    upward = multiply(n_ref[...], wu_ref[...])
    back = times_transposed(b_ref[...], wd_ref[...])
    square = gate * gate
    bend = jnp.tanh(root * gate * (1.0 + 0.044715 * square))
    half_sum = 0.5 * (1.0 + bend)
    activated = gate * half_sum
    slope = half_sum + 0.5 * gate * (1.0 - bend * bend) * (root * (1.0 + 3 * 0.044715 * square))
    hidden = (activated * upward).astype(jnp.bfloat16)
    grad_gate = (back * upward * slope).astype(jnp.bfloat16)
    grad_upward = (back * activated).astype(jnp.bfloat16)
    hid_ref[...] = hidden
    gg_ref[...] = grad_gate
    gu_ref[...] = grad_upward
    y_ref[...] += multiply(hidden, wd_ref[...])
    gn_ref[...] += times_transposed(grad_gate, wg_ref[...]) + times_transposed(
        grad_upward, wu_ref[...]
    )


def shape(dims, dtype):
    return jax.ShapeDtypeStruct(tuple(dims), dtype)


def self_attention(q, k, v, counts, base):
    seqs, length = counts.shape[0], q.shape[0] // counts.shape[0]
    wide, narrow = STEP_HEADS * HEAD_SIZE, PAIR * HEAD_SIZE
    return pl.pallas_call(
        self_forward_kernel,
        out_shape=(shape(q.shape, jnp.bfloat16), shape((seqs, PAIRS, 8, length), jnp.float32)),
        grid_spec=pltpu.PrefetchScalarGridSpec(
            num_scalar_prefetch=1,
            grid=(seqs, PAIRS),
            in_specs=[
                pl.BlockSpec((length, wide), lambda s, p, _: (s, p)),
                pl.BlockSpec((length, narrow), lambda s, p, _: (s, p)),
                pl.BlockSpec((length, narrow), lambda s, p, _: (s, p)),
                pl.BlockSpec((1, STEP_HEADS, length), lambda s, p, _: (p, 0, 0)),
            ],
            out_specs=(
                pl.BlockSpec((length, wide), lambda s, p, _: (s, p)),
                pl.BlockSpec((1, 1, 8, length), lambda s, p, _: (s, p, 0, 0)),
            ),
        ),
    )(counts, q, k, v, base)


def self_attention_back(q, k, v, counts, base, lse, gradient):
    seqs, length = counts.shape[0], q.shape[0] // counts.shape[0]
    wide, narrow = STEP_HEADS * HEAD_SIZE, PAIR * HEAD_SIZE
    return pl.pallas_call(
        self_backward_kernel,
        out_shape=(
            shape(q.shape, jnp.bfloat16),
            shape(k.shape, jnp.bfloat16),
            shape(v.shape, jnp.bfloat16),
            shape((seqs, PAIRS, STEP_HEADS, length), jnp.float32),
        ),
        grid_spec=pltpu.PrefetchScalarGridSpec(
            num_scalar_prefetch=1,
            grid=(seqs, PAIRS),
            in_specs=[
                pl.BlockSpec((length, wide), lambda s, p, _: (s, p)),
                pl.BlockSpec((length, narrow), lambda s, p, _: (s, p)),
                pl.BlockSpec((length, narrow), lambda s, p, _: (s, p)),
                pl.BlockSpec((length, wide), lambda s, p, _: (s, p)),
                pl.BlockSpec((1, 1, 8, length), lambda s, p, _: (s, p, 0, 0)),
                pl.BlockSpec((1, STEP_HEADS, length), lambda s, p, _: (p, 0, 0)),
            ],
            out_specs=(
                pl.BlockSpec((length, wide), lambda s, p, _: (s, p)),
                pl.BlockSpec((length, narrow), lambda s, p, _: (s, p)),
                pl.BlockSpec((length, narrow), lambda s, p, _: (s, p)),
                pl.BlockSpec((1, 1, STEP_HEADS, length), lambda s, p, _: (s, p, 0, 0)),
            ),
        ),
    )(counts, q, k, v, gradient, lse, base)


def chunk_specs(pieces):
    rows, narrow = pieces[0].shape[1], PAIR * HEAD_SIZE
    keys = [pl.BlockSpec((1, rows, narrow), lambda s, p, *_: (s, 0, p)) for _ in pieces]
    values = [pl.BlockSpec((1, rows, narrow), lambda s, p, *_: (s, 0, PAIRS + p)) for _ in pieces]
    return keys + values


def cross_attention(q, pieces, counts, bases):
    seqs, length, rows = counts.shape[0], q.shape[0] // counts.shape[0], pieces[0].shape[1]
    wide = STEP_HEADS * HEAD_SIZE
    return pl.pallas_call(
        functools.partial(cross_forward_kernel, len(pieces)),
        out_shape=(shape(q.shape, jnp.bfloat16), shape((seqs, PAIRS, 8, length), jnp.float32)),
        grid_spec=pltpu.PrefetchScalarGridSpec(
            num_scalar_prefetch=2,
            grid=(seqs, PAIRS),
            in_specs=[pl.BlockSpec((length, wide), lambda s, p, *_: (s, p))] + chunk_specs(pieces),
            out_specs=(
                pl.BlockSpec((length, wide), lambda s, p, *_: (s, p)),
                pl.BlockSpec((1, 1, 8, length), lambda s, p, *_: (s, p, 0, 0)),
            ),
            scratch_shapes=[pltpu.VMEM((len(pieces), SHARED * length, rows), jnp.float32)],
        ),
    )(counts, bases, q, *pieces, *pieces)


def cross_attention_back(q, pieces, counts, bases, lse, gradient):
    seqs, length, rows = counts.shape[0], q.shape[0] // counts.shape[0], pieces[0].shape[1]
    wide, chunks = STEP_HEADS * HEAD_SIZE, len(pieces)
    return pl.pallas_call(
        functools.partial(cross_backward_kernel, chunks),
        out_shape=(shape(q.shape, jnp.bfloat16),)
        + tuple(shape(piece.shape, jnp.bfloat16) for piece in pieces),
        grid_spec=pltpu.PrefetchScalarGridSpec(
            num_scalar_prefetch=2,
            grid=(seqs, PAIRS),
            in_specs=[
                pl.BlockSpec((length, wide), lambda s, p, *_: (s, p)),
                pl.BlockSpec((length, wide), lambda s, p, *_: (s, p)),
                pl.BlockSpec((1, 1, 8, length), lambda s, p, *_: (s, p, 0, 0)),
            ]
            + chunk_specs(pieces),
            out_specs=(pl.BlockSpec((length, wide), lambda s, p, *_: (s, p)),)
            + tuple(
                pl.BlockSpec((1,) + piece.shape[1:], lambda s, p, *_: (s, 0, 0)) for piece in pieces
            ),
            scratch_shapes=[pltpu.VMEM((chunks, rows, SHARED * length), jnp.float32)] * 2,
        ),
    )(counts, bases, q, gradient, lse, *pieces, *pieces)


def feed_forward(rows_normed, branch, w_gate, w_up, w_down):
    rows, width = rows_normed.shape
    hidden = w_gate.shape[1]
    tile = 256
    return pl.pallas_call(
        feed_forward_kernel,
        out_shape=(shape((rows, hidden), jnp.bfloat16),) * 3
        + (shape((rows, width), jnp.float32),) * 2,
        grid=(hidden // tile,),
        in_specs=[
            pl.BlockSpec((rows, width), lambda f: (0, 0)),
            pl.BlockSpec((rows, width), lambda f: (0, 0)),
            pl.BlockSpec((width, tile), lambda f: (0, f)),
            pl.BlockSpec((width, tile), lambda f: (0, f)),
            pl.BlockSpec((tile, width), lambda f: (f, 0)),
        ],
        out_specs=(pl.BlockSpec((rows, tile), lambda f: (0, f)),) * 3
        + (pl.BlockSpec((rows, width), lambda f: (0, 0)),) * 2,
    )(rows_normed, branch, w_gate, w_up, w_down)


def bit_count(size):
    return size.bit_length() - 1


def reduce_rows(term, order):
    devices, members = lax.axis_size("dp"), lax.axis_size("mem")
    me, member = lax.axis_index("dp"), lax.axis_index("mem")
    bits = bit_count(devices)
    rows, columns = term.shape
    share = rows // (devices * members)
    current = term.reshape((2,) * bits + (members, share, columns))
    left = list(range(bits - 1, -1, -1))
    for bit in order:
        axis = left.index(bit)
        left.remove(bit)
        mine = (me >> bit) & 1
        sent = lax.dynamic_index_in_dim(current, 1 - mine, axis, keepdims=False)
        got = lax.ppermute(sent, "dp", [(i, i ^ (1 << bit)) for i in range(devices)])
        kept = lax.dynamic_index_in_dim(current, mine, axis, keepdims=False)
        current = (kept.astype(jnp.float32) + got.astype(jnp.float32)).astype(jnp.bfloat16)
    total = lax.dynamic_index_in_dim(current, member, 0, keepdims=False).astype(jnp.float32)
    for sign in (1, -1):
        got = None
        for step in range(members - 1):
            place = member if sign == 1 else members - 1 - member
            block = jnp.clip(members - 1 - step + place, 0, members - 1)
            block = block if sign == 1 else members - 1 - block
            sent = lax.dynamic_index_in_dim(current, block, 0, keepdims=False)
            if got is not None:
                sent = (sent.astype(jnp.float32) + got.astype(jnp.float32)).astype(jnp.bfloat16)
            pairs = [(i, i + 1) for i in range(step + 1)]
            if sign == -1:
                pairs = [(members - 1 - a, members - 1 - b) for a, b in pairs]
            got = lax.ppermute(sent, "mem", pairs)
        total = total + got.astype(jnp.float32)
    return total


LANES = 128


def partner_masks(order):
    stages = len(order)
    masks = []
    for place in range(1 << stages):
        mask = 0
        for stage, bit in enumerate(order):
            if not (place >> (stages - 1 - stage)) & 1:
                mask |= 1 << bit
        masks.append(mask)
    return masks


def outer_kernel(lefts, chunk, segments, orders, me_ref, *refs):
    a_refs, refs = refs[:lefts], refs[lefts:]
    b_refs, refs = refs[: lefts * len(segments)], refs[lefts * len(segments) :]
    outs, refs = refs[: 2 * len(orders)], refs[2 * len(orders) :]
    plain_ref, arranged = refs[0], refs[1:]
    blocks = 1 << len(orders[0])
    block = plain_ref.shape[0] // blocks
    members, share = outs[0].shape[1], outs[0].shape[2] // chunk
    me = me_ref[0]

    @pl.when(pl.program_id(0) == 0)
    def _():
        tokens = a_refs[0].shape[0]
        for index, a_ref in enumerate(a_refs):
            plain_ref[:, index * tokens : (index + 1) * tokens] = jnp.transpose(a_ref[...])
        for order, arranged_ref in zip(orders, arranged):
            for place, mask in enumerate(partner_masks(order)):
                source = pl.multiple_of((me ^ mask) * block, 16)
                arranged_ref[place * block : (place + 1) * block] = plain_ref[
                    pl.ds(source, block)
                ]

    step = 0
    for index, (steps, color) in enumerate(segments):
        rights = b_refs[lefts * index : lefts * (index + 1)]

        @pl.when((pl.program_id(0) >= step) & (pl.program_id(0) < step + steps))
        def _(color=color, rights=rights):
            right = joined([right_ref[...] for right_ref in rights], 0)
            product = multiply(arranged[color][...], right).astype(jnp.bfloat16)
            for place in range(blocks):
                half_ref = outs[2 * color + (0 if place < blocks // 2 else 1)]
                for m in range(members):
                    first = place * block + m * share
                    for tile in range(chunk):
                        half_ref[place % (blocks // 2), m, tile * share : (tile + 1) * share] = (
                            product[first : first + share, tile * LANES : (tile + 1) * LANES]
                        )

        step += steps


def outer_arranged(lefts, parts, orders, chunk):
    tokens, features = lefts[0].shape
    devices, members = lax.axis_size("dp"), lax.axis_size("mem")
    share = features // (devices * members)
    half = devices // 2
    wide = chunk * LANES
    segments, in_specs, operands, step = [], [], [], 0
    totals = [0] * len(orders)
    for rights, first, columns, color in parts:
        steps = columns // wide
        segments.append((steps, color))
        totals[color] += steps
        for right in rights:
            operands.append(right)
            in_specs.append(
                pl.BlockSpec(
                    (tokens, wide),
                    lambda j, _, step=step, steps=steps, first=first: (
                        0,
                        first // wide + jnp.clip(j - step, 0, steps - 1),
                    ),
                )
            )
        step += steps
    out_shape, out_specs, before = [], [], 0
    for total in totals:
        for _ in range(2):
            out_shape.append(shape((half, members, share * chunk * total, LANES), jnp.bfloat16))
            out_specs.append(
                pl.BlockSpec(
                    (half, members, share * chunk, LANES),
                    lambda j, _, before=before, total=total: (
                        0,
                        0,
                        jnp.clip(j - before, 0, total - 1),
                        0,
                    ),
                )
            )
        before += total
    me = lax.axis_index("dp").astype(jnp.int32).reshape(1)
    kernel = functools.partial(
        outer_kernel, len(lefts), chunk, tuple(segments), tuple(tuple(o) for o in orders)
    )
    return pl.pallas_call(
        kernel,
        out_shape=tuple(out_shape),
        grid_spec=pltpu.PrefetchScalarGridSpec(
            num_scalar_prefetch=1,
            grid=(step,),
            in_specs=[pl.BlockSpec((tokens, features), lambda j, _: (0, 0))] * len(lefts) + in_specs,
            out_specs=tuple(out_specs),
            scratch_shapes=[pltpu.VMEM((features, tokens * len(lefts)), jnp.bfloat16)]
            * (1 + len(orders)),
        ),
    )(me, *lefts, *operands)


def project_kernel(members, place_ref, x_ref, ck_ref, cv_ref, *out_refs):
    width = ck_ref.shape[1]
    for index in range(members):

        @pl.when(pl.program_id(0) == index)
        def _(index=index):
            out_ref = out_refs[index]
            rows = x_ref[0].reshape(-1, x_ref.shape[-1])
            kept = out_ref.shape[:2] + (width,)
            out_ref[:, :, :width] = (
                multiply(rows, ck_ref[...]).astype(jnp.bfloat16).reshape(kept)
            )
            out_ref[:, :, width:] = (
                multiply(rows, cv_ref[...]).astype(jnp.bfloat16).reshape(kept)
            )


def project_memory(memory, m, seqs, c_key, c_value):
    members = lax.axis_size("mem")
    _, _, rows, width = memory.shape
    kept = (seqs, rows, c_key.shape[1] + c_value.shape[1])
    me = lax.axis_index("mem").astype(jnp.int32).reshape(1)
    found = pl.pallas_call(
        functools.partial(project_kernel, members),
        out_shape=(shape(kept, jnp.bfloat16),) * members,
        grid_spec=pltpu.PrefetchScalarGridSpec(
            num_scalar_prefetch=1,
            grid=(members,),
            in_specs=[
                pl.BlockSpec(
                    (1, seqs, rows, width),
                    lambda t, me: (m, lax.rem(me[0] + t + 1, members), 0, 0),
                ),
                pl.BlockSpec(c_key.shape, lambda t, _: (0, 0)),
                pl.BlockSpec(c_value.shape, lambda t, _: (0, 0)),
            ],
            out_specs=(pl.BlockSpec(kept, lambda t, _: (0, 0, 0)),) * members,
        ),
    )(me, memory, c_key, c_value)
    return [found[-1]] + list(found[:-1])


def memory_kernel(pieces, orders, place_ref, x_ref, ck_ref, cv_ref, *refs):
    piece_refs, refs = refs[:pieces], refs[pieces:]
    grad_ref, outs, (now_ref, sum_ref) = refs[0], refs[1:5], refs[5:]
    step, width = pl.program_id(0), ck_ref.shape[1]

    @pl.when(step == 0)
    def _():
        sum_ref[...] = jnp.zeros_like(sum_ref)

    for index in range(pieces):

        @pl.when(step == index)
        def _(index=index):
            now_ref[...] = piece_refs[index][...].reshape(now_ref.shape)

    now = now_ref[...]
    grad = times_transposed(now[:, :width], ck_ref[...]) + times_transposed(
        now[:, width:], cv_ref[...]
    )
    grad_ref[0] = grad.astype(jnp.bfloat16).reshape(grad_ref.shape[1:])
    sum_ref[...] += outer_sum(x_ref[0].reshape(-1, x_ref.shape[-1]), now)

    @pl.when(step == pieces - 1)
    def _():
        blocks = 1 << len(orders[0])
        block = sum_ref.shape[0] // blocks
        members = outs[0].shape[1]
        tiles = width // LANES
        share = block // members
        for color, order in enumerate(orders):
            for place, mask in enumerate(partner_masks(order)):
                source = pl.multiple_of((place_ref[0] ^ mask) * block, 8)
                half_ref = outs[2 * color + (0 if place < blocks // 2 else 1)]
                found = sum_ref[pl.ds(source, block), color * width : (color + 1) * width]
                found = found.astype(jnp.bfloat16)
                for m in range(members):
                    for tile in range(tiles):
                        half_ref[place % (blocks // 2), m, tile * share : (tile + 1) * share] = (
                            found[m * share : (m + 1) * share, tile * LANES : (tile + 1) * LANES]
                        )


def memory_backward(memory, pieces, c_key, c_value, orders):
    devices, members = lax.axis_size("dp"), lax.axis_size("mem")
    seqs, rows, both = pieces[0].shape
    width = memory.shape[-1]
    half, share = devices // 2, width // (devices * members)
    kept = (half, members, share * (both // 2 // LANES), LANES)
    place = jnp.stack([lax.axis_index("dp"), lax.axis_index("mem")]).astype(jnp.int32)

    def block_index(t, place):
        return (t // members, lax.rem(place[1] + lax.rem(t, members), members), 0, 0)

    found = pl.pallas_call(
        functools.partial(memory_kernel, len(pieces), tuple(tuple(o) for o in orders)),
        out_shape=(shape(memory.shape, jnp.bfloat16),) + (shape(kept, jnp.bfloat16),) * 4,
        grid_spec=pltpu.PrefetchScalarGridSpec(
            num_scalar_prefetch=1,
            grid=(len(pieces),),
            in_specs=[
                pl.BlockSpec((1, seqs, rows, width), block_index),
                pl.BlockSpec(c_key.shape, lambda t, _: (0, 0)),
                pl.BlockSpec(c_value.shape, lambda t, _: (0, 0)),
            ]
            + [pl.BlockSpec((seqs, rows, both), lambda t, _: (0, 0, 0))] * len(pieces),
            out_specs=(pl.BlockSpec((1, seqs, rows, width), block_index),)
            + (pl.BlockSpec(kept, lambda t, _: (0, 0, 0, 0)),) * 4,
            scratch_shapes=[
                pltpu.VMEM((seqs * rows, both), jnp.bfloat16),
                pltpu.VMEM((width, both), jnp.float32),
            ],
        ),
    )(place, memory, c_key, c_value, *pieces)
    return found[0], found[1:3], found[3:5]


def swap(array, bit):
    size = lax.axis_size("dp")
    return lax.ppermute(array, "dp", [(i, i ^ (1 << bit)) for i in range(size)])


def add16(left, right):
    return (left.astype(jnp.float32) + right.astype(jnp.float32)).astype(jnp.bfloat16)


def joined(arrays, axis):
    return arrays[0] if len(arrays) == 1 else jnp.concatenate(arrays, axis=axis)


def first_swap(pairs, bit):
    return [(swap(sent, bit), kept) for sent, kept in pairs]


def halves_of(pairs):
    half = pairs[0][0].shape[0] // 2
    sent = joined([add16(kept[:half], got[:half]) for got, kept in pairs], 2)
    kept = joined([add16(kept[half:], got[half:]) for got, kept in pairs], 2)
    return sent, kept


def next_stage(pairs, bit):
    sent, kept = halves_of(pairs)
    return [(swap(sent, bit), kept)]


def later_stages(pairs, bits):
    for bit in bits:
        pairs = next_stage(pairs, bit)
    return pairs


def whole_of(pairs):
    return joined([add16(kept, got) for got, kept in pairs], 2)[0]


def along_members(current):
    members, member = lax.axis_size("mem"), lax.axis_index("mem")
    total = lax.dynamic_index_in_dim(current, member, 0, keepdims=False).astype(jnp.float32)
    got = [None, None]
    for step in range(members - 1):
        for side in range(2):
            place = member if side == 0 else members - 1 - member
            block = jnp.clip(members - 1 - step + place, 0, members - 1)
            block = block if side == 0 else members - 1 - block
            sent = lax.dynamic_index_in_dim(current, block, 0, keepdims=False)
            if step:
                sent = add16(sent, got[side])
            pairs = [(i, i + 1) for i in range(step + 1)]
            if side == 1:
                pairs = [(members - 1 - a, members - 1 - b) for a, b in pairs]
            got[side] = lax.ppermute(sent, "mem", pairs)
    return total + got[0].astype(jnp.float32) + got[1].astype(jnp.float32)


def members_sum(pairs):
    flat = [item for pair in pairs for item in pair if item is not None]
    ends = np.cumsum([0] + [item.shape[1] for item in flat])
    total = along_members(jnp.concatenate(flat, axis=1))
    parts = iter([total[ends[i] : ends[i + 1]] for i in range(len(flat))])
    return [tuple(None if item is None else next(parts) for item in pair) for pair in pairs]


def rows_out(total, share, columns, first):
    tiles = columns // LANES
    part = total[first : first + share * tiles].reshape(tiles, share, LANES)
    return part.transpose(1, 0, 2).reshape(share, columns)


def sum_everywhere(value):
    for axis in ("mem", "dp"):
        size = lax.axis_size(axis)
        for bit in range(bit_count(size)):
            value = value + lax.ppermute(value, axis, [(i, i ^ (1 << bit)) for i in range(size)])
    return value


def per_device(
    target_in,
    memory,
    target_len,
    mem_len,
    cotangent,
    gain_self,
    gain_cross,
    gain_ffn,
    rel_table,
    w_query,
    w_key,
    w_value,
    w_out,
    c_query,
    c_key,
    c_value,
    c_out,
    w_gate,
    w_up,
    w_down,
):
    micro, seqs, length, width = target_in.shape
    mem_rows = memory.shape[2]
    members, member = lax.axis_size("mem"), lax.axis_index("mem")
    devices = lax.axis_size("dp")
    bits = bit_count(devices)
    order_a = list(range(bits))
    order_b = [0] + order_a[:0:-1]
    orders = (order_a, order_b)
    count, rows = micro * seqs, seqs * length
    key_width, hidden_width = c_key.shape[1], w_gate.shape[1]
    share, share_down = width // (devices * members), hidden_width // (devices * members)
    half = width // 2
    steps = range(micro)

    def shifted(array, shift):
        return lax.ppermute(array, "mem", [(i, (i + shift) % members) for i in range(members)])

    pieces = []
    for m in steps:
        found = project_memory(memory, m, seqs, c_key, c_value)
        pieces.append([found[0]] + [shifted(found[i], i) for i in range(1, members)])
    bases = jnp.stack(
        [lax.rem(member + members - shift, members) * mem_rows for shift in range(members)]
    ).astype(jnp.int32)

    target_counts = target_len.reshape(count)
    onehot = bucket_onehot(length)
    backwards = onehot[:, (-np.arange(length)) % length]
    base = jnp.dot(rel_table.T, jnp.asarray(onehot), precision=EXACT_PRECISION)
    base = base.reshape(PAIRS, STEP_HEADS, length)
    base_back = jnp.dot(rel_table.T, jnp.asarray(backwards), precision=EXACT_PRECISION)
    base_back = base_back.reshape(PAIRS, STEP_HEADS, length)

    inputs = target_in.reshape(count * length, width).astype(jnp.float32)
    normed_self = normed(inputs, gain_self)
    queries = multiply(normed_self, w_query).astype(jnp.bfloat16)
    keys = multiply(normed_self, w_key).astype(jnp.bfloat16)
    values = multiply(normed_self, w_value).astype(jnp.bfloat16)
    attended, self_lse = self_attention(queries, keys, values, target_counts, base_back)

    position = jnp.arange(length)
    outs, after_selfs, normed_crosses, cross_queries_all, mixed_all = [], [], [], [], []
    normed_ffns, branches_ffn, hiddens, gates, ups = [], [], [], [], []
    branches_cross, grad_queries_cross, branches_self = [], [], []
    grad_after_selfs, grads_attended = [], []
    sum_gain_ffn = sum_gain_cross = 0.0
    for m in steps:
        after_self = inputs[m * rows : (m + 1) * rows] + multiply(
            attended[m * rows : (m + 1) * rows], w_out
        )
        after_selfs.append(after_self)
        normed_crosses.append(normed(after_self, gain_cross))
        cross_queries_all.append(multiply(normed_crosses[m], c_query).astype(jnp.bfloat16))
    grad_pieces = []
    for m in steps:
        after_self, cross_queries = after_selfs[m], cross_queries_all[m]
        memory_counts = mem_len[m]
        cross_mixed, cross_lse = cross_attention(cross_queries, pieces[m], memory_counts, bases)
        mixed_all.append(cross_mixed)
        after_cross = after_self + multiply(cross_mixed, c_out)
        normed_ffn = normed(after_cross, gain_ffn)
        normed_ffns.append(normed_ffn)
        valid = (position[None, :] < target_len[m][:, None]).reshape(rows, 1)
        branch_ffn = jnp.where(valid, cotangent[m].reshape(rows, width), 0)
        branches_ffn.append(branch_ffn)
        grad_result = branch_ffn.astype(jnp.float32)
        hidden, grad_gate, grad_upward, ffn_out, grad_normed = feed_forward(
            normed_ffn, branch_ffn, w_gate, w_up, w_down
        )
        hiddens.append(hidden)
        gates.append(grad_gate)
        ups.append(grad_upward)
        outs.append(jnp.where(valid, after_cross + ffn_out, 0.0).astype(jnp.bfloat16))
        if m == micro - 1:
            gate_pairs = []
            for rights, order in ((gates, order_a), (ups, order_b)):
                found = outer_arranged(
                    normed_ffns,
                    [(rights, 0, hidden_width, 0)],
                    (order,),
                    hidden_width // (2 * LANES),
                )
                found = first_swap([found], 0)
                gate_pairs.append(next_stage(found, order[1]))
            packed_down = share_down % 8 == 0 and (hidden_width // devices) % 16 == 0
            if packed_down:
                found = outer_arranged(
                    hiddens,
                    [(branches_ffn, 0, half, 0), (branches_ffn, half, half, 1)],
                    orders,
                    half // LANES,
                )
                down_pairs = first_swap([found[0:2]], 0), first_swap([found[2:4]], 0)
                down_pairs = [
                    next_stage(pairs, order[1]) for pairs, order in zip(down_pairs, orders)
                ]
        part, gain_part = norm_back(after_cross, gain_ffn, grad_normed)
        sum_gain_ffn = sum_gain_ffn + gain_part
        grad_after_cross = grad_result + part
        branch_cross = grad_after_cross.astype(jnp.bfloat16)
        branches_cross.append(branch_cross)
        grad_cross_mixed = times_transposed(branch_cross, c_out).astype(jnp.bfloat16)
        found = cross_attention_back(
            cross_queries, pieces[m], memory_counts, bases, cross_lse, grad_cross_mixed
        )
        grad_queries_cross.append(found[0])
        for shift in range(members):
            piece = found[1 + shift]
            if shift:
                piece = shifted(piece, members - shift)
            grad_pieces.append(piece)
        part, gain_part = norm_back(
            after_self, gain_cross, times_transposed(found[0], c_query)
        )
        sum_gain_cross = sum_gain_cross + gain_part
        grad_after_self = grad_after_cross + part
        grad_after_selfs.append(grad_after_self)
        branches_self.append(grad_after_self.astype(jnp.bfloat16))
        grads_attended.append(times_transposed(branches_self[m], w_out).astype(jnp.bfloat16))
    chunk = key_width // LANES
    c_out_sum = outer_arranged(mixed_all, [(branches_cross, 0, width, 0)], (order_a,), chunk)
    c_query_sum = outer_arranged(
        normed_crosses, [(grad_queries_cross, 0, width, 0)], (order_b,), chunk
    )
    attended_parts = [attended[m * rows : (m + 1) * rows] for m in steps]
    w_out_sum = outer_arranged(
        attended_parts,
        [(branches_self, 0, half, 0), (branches_self, half, half, 1)],
        orders,
        chunk,
    )
    rest_pairs = (
        first_swap([c_out_sum, w_out_sum[0:2]], 0),
        first_swap([c_query_sum, w_out_sum[2:4]], 0),
    )
    ffn = [[whole_of(later_stages(p, o[2:])) for p, o in zip(gate_pairs, orders)]]
    if packed_down:
        ffn.append([whole_of(later_stages(p, o[2:])) for p, o in zip(down_pairs, orders)])
    rest_pairs = [next_stage(p, o[1]) for p, o in zip(rest_pairs, orders)]
    rest_a, rest_b = [whole_of(later_stages(p, o[2:])) for p, o in zip(rest_pairs, orders)]

    grad_queries, grad_keys, grad_values, diagonals = self_attention_back(
        queries,
        keys,
        values,
        target_counts,
        base,
        self_lse,
        jnp.concatenate(grads_attended, axis=0),
    )
    w_self_sum = outer_arranged(
        [normed_self],
        [
            ([grad_keys], 0, key_width, 0),
            ([grad_queries], 0, width, 1),
            ([grad_values], 0, key_width, 1),
        ],
        orders,
        chunk,
    )
    self_pairs = first_swap([w_self_sum[0:2]], 0), first_swap([w_self_sum[2:4]], 0)
    self_pairs = [next_stage(p, o[1]) for p, o in zip(self_pairs, orders)]
    self_a, self_b = [whole_of(later_stages(p, o[2:])) for p, o in zip(self_pairs, orders)]
    (gate_a, gate_b), (down_a, down_b) = members_sum(ffn + [(None, None)] * (2 - len(ffn)))
    g_gate = rows_out(gate_a, share, hidden_width, 0)
    g_up = rows_out(gate_b, share, hidden_width, 0)
    if packed_down:
        g_down = jnp.concatenate(
            [rows_out(part, share_down, half, 0) for part in (down_a, down_b)], axis=1
        )
    else:
        g_down = reduce_rows(
            outer_sum(jnp.concatenate(hiddens), jnp.concatenate(branches_ffn)).astype(jnp.bfloat16),
            order_a,
        )

    grad_normed = (
        times_transposed(grad_queries, w_query)
        + times_transposed(grad_keys, w_key)
        + times_transposed(grad_values, w_value)
    )
    part, sum_gain_self = norm_back(inputs, gain_self, grad_normed)
    target_grad = (jnp.concatenate(grad_after_selfs, axis=0) + part).astype(jnp.bfloat16)
    distances = jnp.sum(diagonals, axis=0).reshape(QUERY_HEADS, length)
    table = jnp.dot(distances, jnp.asarray(onehot.T), precision=EXACT_PRECISION).T

    memory_grad, memory_a, memory_b = memory_backward(memory, grad_pieces, c_key, c_value, orders)
    pairs_a = first_swap([memory_a], 0)
    pairs_b = first_swap([memory_b], 0)
    memory_a = whole_of(later_stages(pairs_a, order_a[1:]))
    memory_b = whole_of(later_stages(pairs_b, order_b[1:]))
    (rest_a, rest_b), (self_a, self_b) = members_sum([(rest_a, rest_b), (self_a, self_b)])
    ((memory_a, memory_b),) = members_sum([(memory_a, memory_b)])
    tile_rows = share * (width // LANES)
    g_c_out = rows_out(rest_a, share, width, 0)
    g_c_query = rows_out(rest_b, share, width, 0)
    g_w_out = jnp.concatenate(
        [rows_out(part, share, half, tile_rows) for part in (rest_a, rest_b)], axis=1
    )
    g_w_key = rows_out(self_a, share, key_width, 0)
    g_w_query = rows_out(self_b, share, width, 0)
    g_w_value = rows_out(self_b, share, key_width, tile_rows)
    g_c_key = rows_out(memory_a, share, key_width, 0)
    g_c_value = rows_out(memory_b, share, key_width, 0)

    small = sum_everywhere(
        jnp.concatenate([sum_gain_self, sum_gain_cross, sum_gain_ffn, table.reshape(-1)])
    )
    return (
        jnp.stack(outs).reshape(micro, seqs, length, width),
        target_grad.reshape(micro, seqs, length, width),
        memory_grad,
        small[:width],
        small[width : 2 * width],
        small[2 * width : 3 * width],
        small[3 * width :].reshape(NB, QUERY_HEADS),
        g_w_query,
        g_w_key,
        g_w_value,
        g_w_out,
        g_c_query,
        g_c_key,
        g_c_value,
        g_c_out,
        g_gate,
        g_up,
        g_down,
    )


def solution(mesh):
    rows = P(None, ("dp", "mem"), None, None)
    lengths = P(None, ("dp", "mem"))
    encoded = P(None, "dp", "mem", None)
    return jax.shard_map(
        per_device,
        mesh=mesh,
        in_specs=(rows, encoded, lengths, lengths, rows) + (P(),) * 15,
        out_specs=(rows, rows, encoded) + (P(),) * 4 + (P(("dp", "mem"), None),) * 11,
        check_vma=False,
    )
```

```python
import functools

import jax
import jax.numpy as jnp
import numpy as np
from jax import lax
from jax.experimental import pallas as pl
from jax.experimental.pallas import tpu as pltpu
from jax.sharding import PartitionSpec as P


QUERY_HEADS = 16
HEAD_SIZE = 64
KEY_VALUE_HEADS = 8
NB = 32
MAXD = 128
SHARED = QUERY_HEADS // KEY_VALUE_HEADS
PAIR = 2
PAIRS = KEY_VALUE_HEADS // PAIR
STEP_HEADS = PAIR * SHARED

EPSILON = 1e-06
MASKED = -1e30
EXACT_PRECISION = lax.Precision.HIGHEST


def bucket_index(length):
    half = NB // 2
    distance = np.arange(length)
    spread = np.floor(np.log(np.maximum(distance, half) / half) / np.log(MAXD / half) * half)
    return np.where(distance < half, distance, np.minimum(spread + half, NB - 1)).astype(np.int64)


def bucket_onehot(length):
    chosen = bucket_index(length)
    return np.where(chosen[None, :] == np.arange(NB)[:, None], 1.0, 0.0).astype(np.float32)


def inverse_rms(rows):
    return lax.rsqrt(jnp.mean(rows * rows, axis=-1, keepdims=True) + EPSILON)


def normed(rows, gain):
    return (rows * inverse_rms(rows) * gain).astype(jnp.bfloat16)


def norm_back(rows, gain, gradient):
    scale = inverse_rms(rows)
    scaled = gradient * gain
    shared = jnp.mean(scaled * rows, axis=-1, keepdims=True)
    part_rows = scale * scaled - rows * (scale * scale * scale * shared)
    return part_rows, jnp.sum(gradient * rows * scale, axis=0)


def dot32(left, right, dims):
    return lax.dot_general(left, right, (dims, ((), ())), preferred_element_type=jnp.float32)


def multiply(left, right):
    return dot32(left, right, ((1,), (0,)))


def outer_sum(left, right):
    return dot32(left, right, ((0,), (0,)))


def times_transposed(left, right):
    return dot32(left, right, ((1,), (1,)))


def head_rows(ref_rows, key_head):
    first = key_head * SHARED * HEAD_SIZE
    return jnp.concatenate(
        [ref_rows[:, first + i * HEAD_SIZE : first + (i + 1) * HEAD_SIZE] for i in range(SHARED)],
        axis=0,
    )


def head_columns(rows, length):
    return [rows[i * length : (i + 1) * length] for i in range(SHARED)]


def store_log_totals(lse_ref, columns):
    length = columns[0].shape[0]
    lane = lax.broadcasted_iota(jnp.int32, (length, 128), 1)
    packed = jnp.zeros((length, 128), jnp.float32)
    for index, column in enumerate(columns):
        packed = jnp.where(lane == index, column, packed)
    lse_ref[0, 0] = jnp.transpose(packed)[:8]


def self_forward_kernel(count_ref, q_ref, k_ref, v_ref, base_ref, out_ref, lse_ref):
    length = q_ref.shape[0]
    count = count_ref[pl.program_id(0)]
    row = lax.broadcasted_iota(jnp.int32, (length, length), 0)
    column = lax.broadcasted_iota(jnp.int32, (length, length), 1)
    keep = (column <= row) & (column < count)
    keep = jnp.concatenate([keep.astype(jnp.float32)] * SHARED, axis=0) > 0.5
    outs, totals = [], []
    for j in range(PAIR):
        queries = head_rows(q_ref, j)
        keys = k_ref[:, j * HEAD_SIZE : (j + 1) * HEAD_SIZE]
        values = v_ref[:, j * HEAD_SIZE : (j + 1) * HEAD_SIZE]
        bias = jnp.concatenate(
            [
                pltpu.roll(
                    jnp.broadcast_to(base_ref[0, j * SHARED + i : j * SHARED + i + 1, :], (length, length)),
                    0,
                    1,
                    stride=1,
                    stride_axis=0,
                )
                for i in range(SHARED)
            ],
            axis=0,
        )
        scores = jnp.where(keep, times_transposed(queries, keys) + bias, MASKED)
        highest = jnp.max(scores, axis=-1, keepdims=True)
        terms = jnp.exp(scores - highest)
        total = jnp.sum(terms, axis=-1, keepdims=True)
        mixed = multiply(terms.astype(jnp.bfloat16), values) / total
        outs += head_columns(mixed, length)
        totals += head_columns(highest + jnp.log(total), length)
    out_ref[...] = jnp.concatenate(outs, axis=1).astype(jnp.bfloat16)
    store_log_totals(lse_ref, totals)


def diagonal_sums(square):
    length = square.shape[0]
    group = 8
    total = square[:group]
    for first in range(group, length, group):
        total = total + pltpu.roll(square[first : first + group], length - first, 1)
    row = lax.broadcasted_iota(jnp.int32, (group, length), 0)
    sums = jnp.where(row == 0, total, 0.0)
    for r in range(1, group):
        sums = sums + jnp.where(row == r, pltpu.roll(total, length - r, 1), 0.0)
    return jnp.sum(sums, axis=0, keepdims=True)


def self_backward_kernel(
    count_ref, q_ref, k_ref, v_ref, g_ref, lse_ref, base_ref, dq_ref, dk_ref, dv_ref, diag_ref
):
    length = q_ref.shape[0]
    count = count_ref[pl.program_id(0)]
    row = lax.broadcasted_iota(jnp.int32, (length, length), 0)
    column = lax.broadcasted_iota(jnp.int32, (length, length), 1)
    keep = (row <= column) & (row < count)
    dqs, dks, dvs, diagonals = [], [], [], []
    for j in range(PAIR):
        queries = head_rows(q_ref, j)
        gradient = head_rows(g_ref, j)
        keys = k_ref[:, j * HEAD_SIZE : (j + 1) * HEAD_SIZE]
        values = v_ref[:, j * HEAD_SIZE : (j + 1) * HEAD_SIZE]
        scores_all = times_transposed(keys, queries)
        grad_all = times_transposed(values, gradient)
        weights, score_grads = [], []
        for i in range(SHARED):
            h = j * SHARED + i
            bias = pltpu.roll(
                jnp.broadcast_to(base_ref[0, h : h + 1, :], (length, length)),
                0,
                1,
                stride=1,
                stride_axis=0,
            )
            scores = scores_all[:, i * length : (i + 1) * length] + bias
            scores = jnp.where(keep, scores, MASKED)
            probs = jnp.exp(scores - lse_ref[0, 0, h : h + 1, :])
            weights.append(probs.astype(jnp.bfloat16))
            product = probs * grad_all[:, i * length : (i + 1) * length]
            centre = jnp.sum(product, axis=0, keepdims=True)
            score_grad = (product - probs * centre).astype(jnp.bfloat16)
            score_grads.append(score_grad)
            diagonals.append(diagonal_sums(score_grad.astype(jnp.float32)))
        weights = jnp.concatenate(weights, axis=1)
        score_grads = jnp.concatenate(score_grads, axis=1)
        dvs.append(multiply(weights, gradient))
        dks.append(multiply(score_grads, queries))
        dq = jnp.transpose(outer_sum(keys, score_grads))
        dqs += head_columns(dq, length)
    dq_ref[...] = jnp.concatenate(dqs, axis=1).astype(jnp.bfloat16)
    dk_ref[...] = jnp.concatenate(dks, axis=1).astype(jnp.bfloat16)
    dv_ref[...] = jnp.concatenate(dvs, axis=1).astype(jnp.bfloat16)
    diag_ref[0, 0] = jnp.concatenate(diagonals, axis=0)


def cross_forward_kernel(chunks, count_ref, base_ref, q_ref, *refs):
    k_refs, v_refs = refs[:chunks], refs[chunks : 2 * chunks]
    out_ref, lse_ref, score_ref = refs[2 * chunks :]
    length, rows = q_ref.shape[0], k_refs[0].shape[1]
    count = count_ref[pl.program_id(0)]
    column = lax.broadcasted_iota(jnp.int32, (1, rows), 1)
    outs, totals = [], []
    for j in range(PAIR):
        queries = head_rows(q_ref, j)
        highest = None
        for c in range(chunks):
            keys = k_refs[c][0, :, j * HEAD_SIZE : (j + 1) * HEAD_SIZE]
            scores = jnp.where(
                column + base_ref[c] < count, times_transposed(queries, keys), MASKED
            )
            score_ref[c] = scores
            top = jnp.max(scores, axis=-1, keepdims=True)
            highest = top if highest is None else jnp.maximum(highest, top)
        total, mixed = 0.0, 0.0
        for c in range(chunks):
            values = v_refs[c][0, :, j * HEAD_SIZE : (j + 1) * HEAD_SIZE]
            terms = jnp.exp(score_ref[c] - highest)
            total = total + jnp.sum(terms, axis=-1, keepdims=True)
            mixed = mixed + multiply(terms.astype(jnp.bfloat16), values)
        outs += head_columns(mixed / total, length)
        totals += head_columns(highest + jnp.log(total), length)
    out_ref[...] = jnp.concatenate(outs, axis=1).astype(jnp.bfloat16)
    store_log_totals(lse_ref, totals)


def cross_backward_kernel(chunks, count_ref, base_ref, q_ref, g_ref, lse_ref, *refs):
    k_refs, v_refs = refs[:chunks], refs[chunks : 2 * chunks]
    dq_ref = refs[2 * chunks]
    d_refs = refs[2 * chunks + 1 : 3 * chunks + 1]
    probs_ref, product_ref = refs[3 * chunks + 1 :]
    length, rows = q_ref.shape[0], k_refs[0].shape[1]
    half = d_refs[0].shape[2] // 2
    count = count_ref[pl.program_id(0)]
    first = pl.program_id(1) * (PAIR * HEAD_SIZE)
    position = lax.broadcasted_iota(jnp.int32, (rows, 1), 0)
    dqs = []
    dks, dvs = [[] for _ in range(chunks)], [[] for _ in range(chunks)]
    for j in range(PAIR):
        queries = head_rows(q_ref, j)
        gradient = head_rows(g_ref, j)
        log_total = jnp.concatenate(
            [lse_ref[0, 0, j * SHARED + i : j * SHARED + i + 1, :] for i in range(SHARED)], axis=1
        )
        centre = 0.0
        for c in range(chunks):
            keys = k_refs[c][0, :, j * HEAD_SIZE : (j + 1) * HEAD_SIZE]
            values = v_refs[c][0, :, j * HEAD_SIZE : (j + 1) * HEAD_SIZE]
            scores = jnp.where(
                position + base_ref[c] < count, times_transposed(keys, queries), MASKED
            )
            probs = jnp.exp(scores - log_total)
            product = probs * times_transposed(values, gradient)
            centre = centre + jnp.sum(product, axis=0, keepdims=True)
            dvs[c].append(multiply(probs.astype(jnp.bfloat16), gradient))
            probs_ref[c] = probs
            product_ref[c] = product
        dq = 0.0
        for c in range(chunks):
            keys = k_refs[c][0, :, j * HEAD_SIZE : (j + 1) * HEAD_SIZE]
            score_grad = (product_ref[c] - probs_ref[c] * centre).astype(jnp.bfloat16)
            dks[c].append(multiply(score_grad, queries))
            dq = dq + outer_sum(keys, score_grad)
        dqs += head_columns(jnp.transpose(dq), length)
    dq_ref[...] = jnp.concatenate(dqs, axis=1).astype(jnp.bfloat16)
    for c in range(chunks):
        d_refs[c][0, :, pl.ds(pl.multiple_of(first, 128), 128)] = jnp.concatenate(
            dks[c], axis=1
        ).astype(jnp.bfloat16)
        d_refs[c][0, :, pl.ds(pl.multiple_of(half + first, 128), 128)] = jnp.concatenate(
            dvs[c], axis=1
        ).astype(jnp.bfloat16)


def feed_forward_kernel(
    n_ref, b_ref, wg_ref, wu_ref, wd_ref, hid_ref, gg_ref, gu_ref, y_ref, gn_ref
):
    root = float(np.sqrt(2.0 / np.pi))

    @pl.when(pl.program_id(0) == 0)
    def _():
        y_ref[...] = jnp.zeros_like(y_ref)
        gn_ref[...] = jnp.zeros_like(gn_ref)

    gate = multiply(n_ref[...], wg_ref[...])
    upward = multiply(n_ref[...], wu_ref[...])
    back = times_transposed(b_ref[...], wd_ref[...])
    square = gate * gate
    bend = jnp.tanh(root * gate * (1.0 + 0.044715 * square))
    half_sum = 0.5 * (1.0 + bend)
    activated = gate * half_sum
    slope = half_sum + 0.5 * gate * (1.0 - bend * bend) * (root * (1.0 + 3 * 0.044715 * square))
    hidden = (activated * upward).astype(jnp.bfloat16)
    grad_gate = (back * upward * slope).astype(jnp.bfloat16)
    grad_upward = (back * activated).astype(jnp.bfloat16)
    hid_ref[...] = hidden
    gg_ref[...] = grad_gate
    gu_ref[...] = grad_upward
    y_ref[...] += multiply(hidden, wd_ref[...])
    gn_ref[...] += times_transposed(grad_gate, wg_ref[...]) + times_transposed(
        grad_upward, wu_ref[...]
    )


def shape(dims, dtype):
    return jax.ShapeDtypeStruct(tuple(dims), dtype)


def self_attention(q, k, v, counts, base):
    seqs, length = counts.shape[0], q.shape[0] // counts.shape[0]
    wide, narrow = STEP_HEADS * HEAD_SIZE, PAIR * HEAD_SIZE
    return pl.pallas_call(
        self_forward_kernel,
        out_shape=(shape(q.shape, jnp.bfloat16), shape((seqs, PAIRS, 8, length), jnp.float32)),
        grid_spec=pltpu.PrefetchScalarGridSpec(
            num_scalar_prefetch=1,
            grid=(seqs, PAIRS),
            in_specs=[
                pl.BlockSpec((length, wide), lambda s, p, _: (s, p)),
                pl.BlockSpec((length, narrow), lambda s, p, _: (s, p)),
                pl.BlockSpec((length, narrow), lambda s, p, _: (s, p)),
                pl.BlockSpec((1, STEP_HEADS, length), lambda s, p, _: (p, 0, 0)),
            ],
            out_specs=(
                pl.BlockSpec((length, wide), lambda s, p, _: (s, p)),
                pl.BlockSpec((1, 1, 8, length), lambda s, p, _: (s, p, 0, 0)),
            ),
        ),
    )(counts, q, k, v, base)


def self_attention_back(q, k, v, counts, base, lse, gradient):
    seqs, length = counts.shape[0], q.shape[0] // counts.shape[0]
    wide, narrow = STEP_HEADS * HEAD_SIZE, PAIR * HEAD_SIZE
    return pl.pallas_call(
        self_backward_kernel,
        out_shape=(
            shape(q.shape, jnp.bfloat16),
            shape(k.shape, jnp.bfloat16),
            shape(v.shape, jnp.bfloat16),
            shape((seqs, PAIRS, STEP_HEADS, length), jnp.float32),
        ),
        grid_spec=pltpu.PrefetchScalarGridSpec(
            num_scalar_prefetch=1,
            grid=(seqs, PAIRS),
            in_specs=[
                pl.BlockSpec((length, wide), lambda s, p, _: (s, p)),
                pl.BlockSpec((length, narrow), lambda s, p, _: (s, p)),
                pl.BlockSpec((length, narrow), lambda s, p, _: (s, p)),
                pl.BlockSpec((length, wide), lambda s, p, _: (s, p)),
                pl.BlockSpec((1, 1, 8, length), lambda s, p, _: (s, p, 0, 0)),
                pl.BlockSpec((1, STEP_HEADS, length), lambda s, p, _: (p, 0, 0)),
            ],
            out_specs=(
                pl.BlockSpec((length, wide), lambda s, p, _: (s, p)),
                pl.BlockSpec((length, narrow), lambda s, p, _: (s, p)),
                pl.BlockSpec((length, narrow), lambda s, p, _: (s, p)),
                pl.BlockSpec((1, 1, STEP_HEADS, length), lambda s, p, _: (s, p, 0, 0)),
            ),
        ),
    )(counts, q, k, v, gradient, lse, base)


def chunk_specs(pieces):
    rows, narrow = pieces[0].shape[1], PAIR * HEAD_SIZE
    keys = [pl.BlockSpec((1, rows, narrow), lambda s, p, *_: (s, 0, p)) for _ in pieces]
    values = [pl.BlockSpec((1, rows, narrow), lambda s, p, *_: (s, 0, PAIRS + p)) for _ in pieces]
    return keys + values


def cross_attention(q, pieces, counts, bases):
    seqs, length, rows = counts.shape[0], q.shape[0] // counts.shape[0], pieces[0].shape[1]
    wide = STEP_HEADS * HEAD_SIZE
    return pl.pallas_call(
        functools.partial(cross_forward_kernel, len(pieces)),
        out_shape=(shape(q.shape, jnp.bfloat16), shape((seqs, PAIRS, 8, length), jnp.float32)),
        grid_spec=pltpu.PrefetchScalarGridSpec(
            num_scalar_prefetch=2,
            grid=(seqs, PAIRS),
            in_specs=[pl.BlockSpec((length, wide), lambda s, p, *_: (s, p))] + chunk_specs(pieces),
            out_specs=(
                pl.BlockSpec((length, wide), lambda s, p, *_: (s, p)),
                pl.BlockSpec((1, 1, 8, length), lambda s, p, *_: (s, p, 0, 0)),
            ),
            scratch_shapes=[pltpu.VMEM((len(pieces), SHARED * length, rows), jnp.float32)],
        ),
    )(counts, bases, q, *pieces, *pieces)


def cross_attention_back(q, pieces, counts, bases, lse, gradient):
    seqs, length, rows = counts.shape[0], q.shape[0] // counts.shape[0], pieces[0].shape[1]
    wide, chunks = STEP_HEADS * HEAD_SIZE, len(pieces)
    return pl.pallas_call(
        functools.partial(cross_backward_kernel, chunks),
        out_shape=(shape(q.shape, jnp.bfloat16),)
        + tuple(shape(piece.shape, jnp.bfloat16) for piece in pieces),
        grid_spec=pltpu.PrefetchScalarGridSpec(
            num_scalar_prefetch=2,
            grid=(seqs, PAIRS),
            in_specs=[
                pl.BlockSpec((length, wide), lambda s, p, *_: (s, p)),
                pl.BlockSpec((length, wide), lambda s, p, *_: (s, p)),
                pl.BlockSpec((1, 1, 8, length), lambda s, p, *_: (s, p, 0, 0)),
            ]
            + chunk_specs(pieces),
            out_specs=(pl.BlockSpec((length, wide), lambda s, p, *_: (s, p)),)
            + tuple(
                pl.BlockSpec((1,) + piece.shape[1:], lambda s, p, *_: (s, 0, 0)) for piece in pieces
            ),
            scratch_shapes=[pltpu.VMEM((chunks, rows, SHARED * length), jnp.float32)] * 2,
        ),
    )(counts, bases, q, gradient, lse, *pieces, *pieces)


def feed_forward(rows_normed, branch, w_gate, w_up, w_down):
    rows, width = rows_normed.shape
    hidden = w_gate.shape[1]
    tile = 256
    return pl.pallas_call(
        feed_forward_kernel,
        out_shape=(shape((rows, hidden), jnp.bfloat16),) * 3
        + (shape((rows, width), jnp.float32),) * 2,
        grid=(hidden // tile,),
        in_specs=[
            pl.BlockSpec((rows, width), lambda f: (0, 0)),
            pl.BlockSpec((rows, width), lambda f: (0, 0)),
            pl.BlockSpec((width, tile), lambda f: (0, f)),
            pl.BlockSpec((width, tile), lambda f: (0, f)),
            pl.BlockSpec((tile, width), lambda f: (f, 0)),
        ],
        out_specs=(pl.BlockSpec((rows, tile), lambda f: (0, f)),) * 3
        + (pl.BlockSpec((rows, width), lambda f: (0, 0)),) * 2,
    )(rows_normed, branch, w_gate, w_up, w_down)


def bit_count(size):
    return size.bit_length() - 1


def reduce_rows(term, order):
    devices, members = lax.axis_size("dp"), lax.axis_size("mem")
    me, member = lax.axis_index("dp"), lax.axis_index("mem")
    bits = bit_count(devices)
    rows, columns = term.shape
    share = rows // (devices * members)
    current = term.reshape((2,) * bits + (members, share, columns))
    left = list(range(bits - 1, -1, -1))
    for bit in order:
        axis = left.index(bit)
        left.remove(bit)
        mine = (me >> bit) & 1
        sent = lax.dynamic_index_in_dim(current, 1 - mine, axis, keepdims=False)
        got = lax.ppermute(sent, "dp", [(i, i ^ (1 << bit)) for i in range(devices)])
        kept = lax.dynamic_index_in_dim(current, mine, axis, keepdims=False)
        current = (kept.astype(jnp.float32) + got.astype(jnp.float32)).astype(jnp.bfloat16)
    total = lax.dynamic_index_in_dim(current, member, 0, keepdims=False).astype(jnp.float32)
    for sign in (1, -1):
        got = None
        for step in range(members - 1):
            place = member if sign == 1 else members - 1 - member
            block = jnp.clip(members - 1 - step + place, 0, members - 1)
            block = block if sign == 1 else members - 1 - block
            sent = lax.dynamic_index_in_dim(current, block, 0, keepdims=False)
            if got is not None:
                sent = (sent.astype(jnp.float32) + got.astype(jnp.float32)).astype(jnp.bfloat16)
            pairs = [(i, i + 1) for i in range(step + 1)]
            if sign == -1:
                pairs = [(members - 1 - a, members - 1 - b) for a, b in pairs]
            got = lax.ppermute(sent, "mem", pairs)
        total = total + got.astype(jnp.float32)
    return total


LANES = 128


def partner_masks(order):
    stages = len(order)
    masks = []
    for place in range(1 << stages):
        mask = 0
        for stage, bit in enumerate(order):
            if not (place >> (stages - 1 - stage)) & 1:
                mask |= 1 << bit
        masks.append(mask)
    return masks


def outer_kernel(lefts, chunk, segments, orders, me_ref, *refs):
    a_refs, refs = refs[:lefts], refs[lefts:]
    b_refs, refs = refs[: lefts * len(segments)], refs[lefts * len(segments) :]
    outs, refs = refs[: 2 * len(orders)], refs[2 * len(orders) :]
    plain_ref, arranged = refs[0], refs[1:]
    blocks = 1 << len(orders[0])
    block = plain_ref.shape[0] // blocks
    members, share = outs[0].shape[1], outs[0].shape[2] // chunk
    me = me_ref[0]

    @pl.when(pl.program_id(0) == 0)
    def _():
        tokens = a_refs[0].shape[0]
        for index, a_ref in enumerate(a_refs):
            plain_ref[:, index * tokens : (index + 1) * tokens] = jnp.transpose(a_ref[...])
        for order, arranged_ref in zip(orders, arranged):
            for place, mask in enumerate(partner_masks(order)):
                source = pl.multiple_of((me ^ mask) * block, 16)
                arranged_ref[place * block : (place + 1) * block] = plain_ref[
                    pl.ds(source, block)
                ]

    step = 0
    for index, (steps, color) in enumerate(segments):
        rights = b_refs[lefts * index : lefts * (index + 1)]

        @pl.when((pl.program_id(0) >= step) & (pl.program_id(0) < step + steps))
        def _(color=color, rights=rights):
            right = joined([right_ref[...] for right_ref in rights], 0)
            product = multiply(arranged[color][...], right).astype(jnp.bfloat16)
            for place in range(blocks):
                half_ref = outs[2 * color + (0 if place < blocks // 2 else 1)]
                for m in range(members):
                    first = place * block + m * share
                    for tile in range(chunk):
                        half_ref[place % (blocks // 2), m, tile * share : (tile + 1) * share] = (
                            product[first : first + share, tile * LANES : (tile + 1) * LANES]
                        )

        step += steps


def outer_arranged(lefts, parts, orders, chunk):
    tokens, features = lefts[0].shape
    devices, members = lax.axis_size("dp"), lax.axis_size("mem")
    share = features // (devices * members)
    half = devices // 2
    wide = chunk * LANES
    segments, in_specs, operands, step = [], [], [], 0
    totals = [0] * len(orders)
    for rights, first, columns, color in parts:
        steps = columns // wide
        segments.append((steps, color))
        totals[color] += steps
        for right in rights:
            operands.append(right)
            in_specs.append(
                pl.BlockSpec(
                    (tokens, wide),
                    lambda j, _, step=step, steps=steps, first=first: (
                        0,
                        first // wide + jnp.clip(j - step, 0, steps - 1),
                    ),
                )
            )
        step += steps
    out_shape, out_specs, before = [], [], 0
    for total in totals:
        for _ in range(2):
            out_shape.append(shape((half, members, share * chunk * total, LANES), jnp.bfloat16))
            out_specs.append(
                pl.BlockSpec(
                    (half, members, share * chunk, LANES),
                    lambda j, _, before=before, total=total: (
                        0,
                        0,
                        jnp.clip(j - before, 0, total - 1),
                        0,
                    ),
                )
            )
        before += total
    me = lax.axis_index("dp").astype(jnp.int32).reshape(1)
    kernel = functools.partial(
        outer_kernel, len(lefts), chunk, tuple(segments), tuple(tuple(o) for o in orders)
    )
    return pl.pallas_call(
        kernel,
        out_shape=tuple(out_shape),
        grid_spec=pltpu.PrefetchScalarGridSpec(
            num_scalar_prefetch=1,
            grid=(step,),
            in_specs=[pl.BlockSpec((tokens, features), lambda j, _: (0, 0))] * len(lefts) + in_specs,
            out_specs=tuple(out_specs),
            scratch_shapes=[pltpu.VMEM((features, tokens * len(lefts)), jnp.bfloat16)]
            * (1 + len(orders)),
        ),
    )(me, *lefts, *operands)


def project_kernel(members, place_ref, x_ref, ck_ref, cv_ref, *out_refs):
    width = ck_ref.shape[1]
    for index in range(members):

        @pl.when(pl.program_id(0) == index)
        def _(index=index):
            out_ref = out_refs[index]
            rows = x_ref[0].reshape(-1, x_ref.shape[-1])
            kept = out_ref.shape[:2] + (width,)
            out_ref[:, :, :width] = (
                multiply(rows, ck_ref[...]).astype(jnp.bfloat16).reshape(kept)
            )
            out_ref[:, :, width:] = (
                multiply(rows, cv_ref[...]).astype(jnp.bfloat16).reshape(kept)
            )


def project_memory(memory, m, seqs, c_key, c_value):
    members = lax.axis_size("mem")
    _, _, rows, width = memory.shape
    kept = (seqs, rows, c_key.shape[1] + c_value.shape[1])
    me = lax.axis_index("mem").astype(jnp.int32).reshape(1)
    found = pl.pallas_call(
        functools.partial(project_kernel, members),
        out_shape=(shape(kept, jnp.bfloat16),) * members,
        grid_spec=pltpu.PrefetchScalarGridSpec(
            num_scalar_prefetch=1,
            grid=(members,),
            in_specs=[
                pl.BlockSpec(
                    (1, seqs, rows, width),
                    lambda t, me: (m, lax.rem(me[0] + t + 1, members), 0, 0),
                ),
                pl.BlockSpec(c_key.shape, lambda t, _: (0, 0)),
                pl.BlockSpec(c_value.shape, lambda t, _: (0, 0)),
            ],
            out_specs=(pl.BlockSpec(kept, lambda t, _: (0, 0, 0)),) * members,
        ),
    )(me, memory, c_key, c_value)
    return [found[-1]] + list(found[:-1])


def memory_kernel(pieces, orders, place_ref, x_ref, ck_ref, cv_ref, *refs):
    piece_refs, refs = refs[:pieces], refs[pieces:]
    grad_ref, outs, (now_ref, sum_ref) = refs[0], refs[1:5], refs[5:]
    step, width = pl.program_id(0), ck_ref.shape[1]

    @pl.when(step == 0)
    def _():
        sum_ref[...] = jnp.zeros_like(sum_ref)

    for index in range(pieces):

        @pl.when(step == index)
        def _(index=index):
            now_ref[...] = piece_refs[index][...].reshape(now_ref.shape)

    now = now_ref[...]
    grad = times_transposed(now[:, :width], ck_ref[...]) + times_transposed(
        now[:, width:], cv_ref[...]
    )
    grad_ref[0] = grad.astype(jnp.bfloat16).reshape(grad_ref.shape[1:])
    sum_ref[...] += outer_sum(x_ref[0].reshape(-1, x_ref.shape[-1]), now)

    @pl.when(step == pieces - 1)
    def _():
        blocks = 1 << len(orders[0])
        block = sum_ref.shape[0] // blocks
        members = outs[0].shape[1]
        tiles = width // LANES
        share = block // members
        for color, order in enumerate(orders):
            for place, mask in enumerate(partner_masks(order)):
                source = pl.multiple_of((place_ref[0] ^ mask) * block, 8)
                half_ref = outs[2 * color + (0 if place < blocks // 2 else 1)]
                found = sum_ref[pl.ds(source, block), color * width : (color + 1) * width]
                found = found.astype(jnp.bfloat16)
                for m in range(members):
                    for tile in range(tiles):
                        half_ref[place % (blocks // 2), m, tile * share : (tile + 1) * share] = (
                            found[m * share : (m + 1) * share, tile * LANES : (tile + 1) * LANES]
                        )


def memory_backward(memory, pieces, c_key, c_value, orders):
    devices, members = lax.axis_size("dp"), lax.axis_size("mem")
    seqs, rows, both = pieces[0].shape
    width = memory.shape[-1]
    half, share = devices // 2, width // (devices * members)
    kept = (half, members, share * (both // 2 // LANES), LANES)
    place = jnp.stack([lax.axis_index("dp"), lax.axis_index("mem")]).astype(jnp.int32)

    def block_index(t, place):
        return (t // members, lax.rem(place[1] + lax.rem(t, members), members), 0, 0)

    found = pl.pallas_call(
        functools.partial(memory_kernel, len(pieces), tuple(tuple(o) for o in orders)),
        out_shape=(shape(memory.shape, jnp.bfloat16),) + (shape(kept, jnp.bfloat16),) * 4,
        grid_spec=pltpu.PrefetchScalarGridSpec(
            num_scalar_prefetch=1,
            grid=(len(pieces),),
            in_specs=[
                pl.BlockSpec((1, seqs, rows, width), block_index),
                pl.BlockSpec(c_key.shape, lambda t, _: (0, 0)),
                pl.BlockSpec(c_value.shape, lambda t, _: (0, 0)),
            ]
            + [pl.BlockSpec((seqs, rows, both), lambda t, _: (0, 0, 0))] * len(pieces),
            out_specs=(pl.BlockSpec((1, seqs, rows, width), block_index),)
            + (pl.BlockSpec(kept, lambda t, _: (0, 0, 0, 0)),) * 4,
            scratch_shapes=[
                pltpu.VMEM((seqs * rows, both), jnp.bfloat16),
                pltpu.VMEM((width, both), jnp.float32),
            ],
        ),
    )(place, memory, c_key, c_value, *pieces)
    return found[0], found[1:3], found[3:5]


def swap(array, bit):
    size = lax.axis_size("dp")
    return lax.ppermute(array, "dp", [(i, i ^ (1 << bit)) for i in range(size)])


def add16(left, right):
    return (left.astype(jnp.float32) + right.astype(jnp.float32)).astype(jnp.bfloat16)


def joined(arrays, axis):
    return arrays[0] if len(arrays) == 1 else jnp.concatenate(arrays, axis=axis)


def first_swap(pairs, bit):
    return [(swap(sent, bit), kept) for sent, kept in pairs]


def halves_of(pairs):
    half = pairs[0][0].shape[0] // 2
    sent = joined([add16(kept[:half], got[:half]) for got, kept in pairs], 2)
    kept = joined([add16(kept[half:], got[half:]) for got, kept in pairs], 2)
    return sent, kept


def next_stage(pairs, bit):
    sent, kept = halves_of(pairs)
    return [(swap(sent, bit), kept)]


def later_stages(pairs, bits):
    for bit in bits:
        pairs = next_stage(pairs, bit)
    return pairs


def whole_of(pairs):
    return joined([add16(kept, got) for got, kept in pairs], 2)[0]


def along_members(current):
    members, member = lax.axis_size("mem"), lax.axis_index("mem")
    total = lax.dynamic_index_in_dim(current, member, 0, keepdims=False).astype(jnp.float32)
    got = [None, None]
    for step in range(members - 1):
        for side in range(2):
            place = member if side == 0 else members - 1 - member
            block = jnp.clip(members - 1 - step + place, 0, members - 1)
            block = block if side == 0 else members - 1 - block
            sent = lax.dynamic_index_in_dim(current, block, 0, keepdims=False)
            if step:
                sent = add16(sent, got[side])
            pairs = [(i, i + 1) for i in range(step + 1)]
            if side == 1:
                pairs = [(members - 1 - a, members - 1 - b) for a, b in pairs]
            got[side] = lax.ppermute(sent, "mem", pairs)
    return total + got[0].astype(jnp.float32) + got[1].astype(jnp.float32)


def members_sum(pairs):
    flat = [item for pair in pairs for item in pair if item is not None]
    ends = np.cumsum([0] + [item.shape[1] for item in flat])
    total = along_members(jnp.concatenate(flat, axis=1))
    parts = iter([total[ends[i] : ends[i + 1]] for i in range(len(flat))])
    return [tuple(None if item is None else next(parts) for item in pair) for pair in pairs]


def rows_out(total, share, columns, first):
    tiles = columns // LANES
    part = total[first : first + share * tiles].reshape(tiles, share, LANES)
    return part.transpose(1, 0, 2).reshape(share, columns)


def sum_everywhere(value):
    for axis in ("mem", "dp"):
        size = lax.axis_size(axis)
        for bit in range(bit_count(size)):
            value = value + lax.ppermute(value, axis, [(i, i ^ (1 << bit)) for i in range(size)])
    return value


def per_device(
    target_in,
    memory,
    target_len,
    mem_len,
    cotangent,
    gain_self,
    gain_cross,
    gain_ffn,
    rel_table,
    w_query,
    w_key,
    w_value,
    w_out,
    c_query,
    c_key,
    c_value,
    c_out,
    w_gate,
    w_up,
    w_down,
):
    micro, seqs, length, width = target_in.shape
    mem_rows = memory.shape[2]
    members, member = lax.axis_size("mem"), lax.axis_index("mem")
    devices = lax.axis_size("dp")
    bits = bit_count(devices)
    order_a = list(range(bits))
    order_b = [0] + order_a[:0:-1]
    orders = (order_a, order_b)
    count, rows = micro * seqs, seqs * length
    key_width, hidden_width = c_key.shape[1], w_gate.shape[1]
    share, share_down = width // (devices * members), hidden_width // (devices * members)
    half = width // 2
    steps = range(micro)

    def shifted(array, shift):
        return lax.ppermute(array, "mem", [(i, (i + shift) % members) for i in range(members)])

    pieces = []
    for m in steps:
        found = project_memory(memory, m, seqs, c_key, c_value)
        pieces.append([found[0]] + [shifted(found[i], i) for i in range(1, members)])
    bases = jnp.stack(
        [lax.rem(member + members - shift, members) * mem_rows for shift in range(members)]
    ).astype(jnp.int32)

    target_counts = target_len.reshape(count)
    onehot = bucket_onehot(length)
    backwards = onehot[:, (-np.arange(length)) % length]
    base = jnp.dot(rel_table.T, jnp.asarray(onehot), precision=EXACT_PRECISION)
    base = base.reshape(PAIRS, STEP_HEADS, length)
    base_back = jnp.dot(rel_table.T, jnp.asarray(backwards), precision=EXACT_PRECISION)
    base_back = base_back.reshape(PAIRS, STEP_HEADS, length)

    inputs = target_in.reshape(count * length, width).astype(jnp.float32)
    normed_self = normed(inputs, gain_self)
    queries = multiply(normed_self, w_query).astype(jnp.bfloat16)
    keys = multiply(normed_self, w_key).astype(jnp.bfloat16)
    values = multiply(normed_self, w_value).astype(jnp.bfloat16)
    attended, self_lse = self_attention(queries, keys, values, target_counts, base_back)

    position = jnp.arange(length)
    outs, after_selfs, normed_crosses, cross_queries_all, mixed_all = [], [], [], [], []
    normed_ffns, branches_ffn, hiddens, gates, ups = [], [], [], [], []
    branches_cross, grad_queries_cross, branches_self = [], [], []
    grad_after_selfs, grads_attended = [], []
    sum_gain_ffn = sum_gain_cross = 0.0
    for m in steps:
        after_self = inputs[m * rows : (m + 1) * rows] + multiply(
            attended[m * rows : (m + 1) * rows], w_out
        )
        after_selfs.append(after_self)
        normed_crosses.append(normed(after_self, gain_cross))
        cross_queries_all.append(multiply(normed_crosses[m], c_query).astype(jnp.bfloat16))
    grad_pieces = []
    for m in steps:
        after_self, cross_queries = after_selfs[m], cross_queries_all[m]
        memory_counts = mem_len[m]
        cross_mixed, cross_lse = cross_attention(cross_queries, pieces[m], memory_counts, bases)
        mixed_all.append(cross_mixed)
        after_cross = after_self + multiply(cross_mixed, c_out)
        normed_ffn = normed(after_cross, gain_ffn)
        normed_ffns.append(normed_ffn)
        valid = (position[None, :] < target_len[m][:, None]).reshape(rows, 1)
        branch_ffn = jnp.where(valid, cotangent[m].reshape(rows, width), 0)
        branches_ffn.append(branch_ffn)
        grad_result = branch_ffn.astype(jnp.float32)
        hidden, grad_gate, grad_upward, ffn_out, grad_normed = feed_forward(
            normed_ffn, branch_ffn, w_gate, w_up, w_down
        )
        hiddens.append(hidden)
        gates.append(grad_gate)
        ups.append(grad_upward)
        outs.append(jnp.where(valid, after_cross + ffn_out, 0.0).astype(jnp.bfloat16))
        if m == micro - 1:
            gate_pairs = []
            for rights, order in ((gates, order_a), (ups, order_b)):
                found = outer_arranged(
                    normed_ffns,
                    [(rights, 0, hidden_width, 0)],
                    (order,),
                    hidden_width // (2 * LANES),
                )
                found = first_swap([found], 0)
                gate_pairs.append(next_stage(found, order[1]))
            packed_down = share_down % 8 == 0 and (hidden_width // devices) % 16 == 0
            if packed_down:
                found = outer_arranged(
                    hiddens,
                    [(branches_ffn, 0, half, 0), (branches_ffn, half, half, 1)],
                    orders,
                    half // LANES,
                )
                down_pairs = first_swap([found[0:2]], 0), first_swap([found[2:4]], 0)
                down_pairs = [
                    next_stage(pairs, order[1]) for pairs, order in zip(down_pairs, orders)
                ]
        part, gain_part = norm_back(after_cross, gain_ffn, grad_normed)
        sum_gain_ffn = sum_gain_ffn + gain_part
        grad_after_cross = grad_result + part
        branch_cross = grad_after_cross.astype(jnp.bfloat16)
        branches_cross.append(branch_cross)
        grad_cross_mixed = times_transposed(branch_cross, c_out).astype(jnp.bfloat16)
        found = cross_attention_back(
            cross_queries, pieces[m], memory_counts, bases, cross_lse, grad_cross_mixed
        )
        grad_queries_cross.append(found[0])
        for shift in range(members):
            piece = found[1 + shift]
            if shift:
                piece = shifted(piece, members - shift)
            grad_pieces.append(piece)
        part, gain_part = norm_back(
            after_self, gain_cross, times_transposed(found[0], c_query)
        )
        sum_gain_cross = sum_gain_cross + gain_part
        grad_after_self = grad_after_cross + part
        grad_after_selfs.append(grad_after_self)
        branches_self.append(grad_after_self.astype(jnp.bfloat16))
        grads_attended.append(times_transposed(branches_self[m], w_out).astype(jnp.bfloat16))
    chunk = key_width // LANES
    c_out_sum = outer_arranged(mixed_all, [(branches_cross, 0, width, 0)], (order_a,), chunk)
    c_query_sum = outer_arranged(
        normed_crosses, [(grad_queries_cross, 0, width, 0)], (order_b,), chunk
    )
    attended_parts = [attended[m * rows : (m + 1) * rows] for m in steps]
    w_out_sum = outer_arranged(
        attended_parts,
        [(branches_self, 0, half, 0), (branches_self, half, half, 1)],
        orders,
        chunk,
    )
    rest_pairs = (
        first_swap([c_out_sum, w_out_sum[0:2]], 0),
        first_swap([c_query_sum, w_out_sum[2:4]], 0),
    )
    ffn = [[whole_of(later_stages(p, o[2:])) for p, o in zip(gate_pairs, orders)]]
    if packed_down:
        ffn.append([whole_of(later_stages(p, o[2:])) for p, o in zip(down_pairs, orders)])
    rest_pairs = [next_stage(p, o[1]) for p, o in zip(rest_pairs, orders)]
    rest_a, rest_b = [whole_of(later_stages(p, o[2:])) for p, o in zip(rest_pairs, orders)]

    grad_queries, grad_keys, grad_values, diagonals = self_attention_back(
        queries,
        keys,
        values,
        target_counts,
        base,
        self_lse,
        jnp.concatenate(grads_attended, axis=0),
    )
    w_self_sum = outer_arranged(
        [normed_self],
        [
            ([grad_keys], 0, key_width, 0),
            ([grad_queries], 0, width, 1),
            ([grad_values], 0, key_width, 1),
        ],
        orders,
        chunk,
    )
    self_pairs = first_swap([w_self_sum[0:2]], 0), first_swap([w_self_sum[2:4]], 0)
    self_pairs = [next_stage(p, o[1]) for p, o in zip(self_pairs, orders)]
    self_a, self_b = [whole_of(later_stages(p, o[2:])) for p, o in zip(self_pairs, orders)]
    (gate_a, gate_b), (down_a, down_b) = members_sum(ffn + [(None, None)] * (2 - len(ffn)))
    g_gate = rows_out(gate_a, share, hidden_width, 0)
    g_up = rows_out(gate_b, share, hidden_width, 0)
    if packed_down:
        g_down = jnp.concatenate(
            [rows_out(part, share_down, half, 0) for part in (down_a, down_b)], axis=1
        )
    else:
        g_down = reduce_rows(
            outer_sum(jnp.concatenate(hiddens), jnp.concatenate(branches_ffn)).astype(jnp.bfloat16),
            order_a,
        )

    grad_normed = (
        times_transposed(grad_queries, w_query)
        + times_transposed(grad_keys, w_key)
        + times_transposed(grad_values, w_value)
    )
    part, sum_gain_self = norm_back(inputs, gain_self, grad_normed)
    target_grad = (jnp.concatenate(grad_after_selfs, axis=0) + part).astype(jnp.bfloat16)
    distances = jnp.sum(diagonals, axis=0).reshape(QUERY_HEADS, length)
    table = jnp.dot(distances, jnp.asarray(onehot.T), precision=EXACT_PRECISION).T

    memory_grad, memory_a, memory_b = memory_backward(memory, grad_pieces, c_key, c_value, orders)
    pairs_a = first_swap([memory_a], 0)
    pairs_b = first_swap([memory_b], 0)
    memory_a = whole_of(later_stages(pairs_a, order_a[1:]))
    memory_b = whole_of(later_stages(pairs_b, order_b[1:]))
    (rest_a, rest_b), (self_a, self_b), (memory_a, memory_b) = members_sum(
        [(rest_a, rest_b), (self_a, self_b), (memory_a, memory_b)]
    )
    tile_rows = share * (width // LANES)
    g_c_out = rows_out(rest_a, share, width, 0)
    g_c_query = rows_out(rest_b, share, width, 0)
    g_w_out = jnp.concatenate(
        [rows_out(part, share, half, tile_rows) for part in (rest_a, rest_b)], axis=1
    )
    g_w_key = rows_out(self_a, share, key_width, 0)
    g_w_query = rows_out(self_b, share, width, 0)
    g_w_value = rows_out(self_b, share, key_width, tile_rows)
    g_c_key = rows_out(memory_a, share, key_width, 0)
    g_c_value = rows_out(memory_b, share, key_width, 0)

    small = sum_everywhere(
        jnp.concatenate([sum_gain_self, sum_gain_cross, sum_gain_ffn, table.reshape(-1)])
    )
    return (
        jnp.stack(outs).reshape(micro, seqs, length, width),
        target_grad.reshape(micro, seqs, length, width),
        memory_grad,
        small[:width],
        small[width : 2 * width],
        small[2 * width : 3 * width],
        small[3 * width :].reshape(NB, QUERY_HEADS),
        g_w_query,
        g_w_key,
        g_w_value,
        g_w_out,
        g_c_query,
        g_c_key,
        g_c_value,
        g_c_out,
        g_gate,
        g_up,
        g_down,
    )


def solution(mesh):
    rows = P(None, ("dp", "mem"), None, None)
    lengths = P(None, ("dp", "mem"))
    encoded = P(None, "dp", "mem", None)
    return jax.shard_map(
        per_device,
        mesh=mesh,
        in_specs=(rows, encoded, lengths, lengths, rows) + (P(),) * 15,
        out_specs=(rows, rows, encoded) + (P(),) * 4 + (P(("dp", "mem"), None),) * 11,
        check_vma=False,
    )
```
